256 devices in a mesh: region: 32 (over z, x), tm: 8 (over y, core).
Axes of the slice: x: 4, y: 4, z: 8, core: 2. Of those that a mesh axis runs over, the one named last changes fastest.
Arguments:
- observations: bfloat16 [32, 8, 2048, 512], P('region', 'tm'), may hold values from -160 to 160
- counts: int32 [32, 8], P('region', 'tm'), may hold values from 1 to 8, as said below
- visible: int32 [32, 32], replicated, may hold values 0 or 1
- latents: bfloat16 [32, 32, 512], P('region'), may hold values from -6 to 6
- lat_gain: float32 [512], replicated, may hold values from 0.5 to 1.5
- mlp_gain: float32 [512], replicated, may hold values from 0.5 to 1.5
- w_query: bfloat16 [512, 512], replicated, may hold values from -0.25 to 0.25
- w_keyval: bfloat16 [512, 1024], replicated, may hold values from -0.25 to 0.25
- w_out: bfloat16 [512, 512], replicated, may hold values from -0.25 to 0.25
- w_up: bfloat16 [512, 2048], P(None, 'tm'), may hold values from -0.25 to 0.25
- w_down: bfloat16 [2048, 512], P('tm'), may hold values from -0.125 to 0.125
Outputs:
- encoded: bfloat16 [32, 32, 512], P('region')
The draws below stay inside these ranges and needn't reach their ends.
Inputs may be any that keep to these rules, and one draw needn't show every extreme that they name: `counts`: some region and time slot holds 8 blocks.
All inputs are finite; a program needn't handle non-finite values.
Results may differ from the reference program's by a relative error of at most 0.0055.
The reference program's roundings to bfloat16 on the way (of `keyval`, `normed`, `queries`, `attended`, `normed2` and `hidden`) count: a program that leaves them out, or rounds other values in their place, can miss the bound.
Values may be sent and summed in bfloat16 or wider, within the bound.
No kernel may reach another device: no remote copies, remote signals or barrier semaphores. Data moves between devices by JAX's collectives and lax.ppermute only.
A program may use at most 64 MiB of HBM per device.

```python
import jax
import jax.numpy as jnp
from jax import lax

D = 512
H = 8
HID = 2048
DH = 64
LR = 32
CAP = 8
BLK = 256
REGIONS = 32
SLOTS = 8


def block_counts(key):
    heavy = jax.random.randint(jax.random.fold_in(key, 101), (REGIONS, 1), 0, 4) == 0
    upper = jax.random.randint(jax.random.fold_in(key, 102), (REGIONS, SLOTS), CAP // 2 + 1, CAP + 1)
    blocks = jnp.where(heavy, upper, 1).astype(jnp.int32).reshape(REGIONS * SLOTS)
    chosen = jax.random.randint(jax.random.fold_in(key, 103), (), 0, REGIONS * SLOTS)
    blocks = jnp.where(jnp.arange(REGIONS * SLOTS, dtype=jnp.int32) == chosen, CAP, blocks)
    return blocks.reshape(REGIONS, SLOTS).astype(jnp.int32)


def draw_counts(key, part):
    return block_counts(key)


def draw_observations(key, part):
    shape = (REGIONS, SLOTS, CAP * BLK, D)
    base_key = jax.random.fold_in(key, 201)
    values = jnp.clip(3.0 * jax.random.normal(base_key, shape, jnp.float32), -18.0, 18.0)
    return values.astype(jnp.bfloat16)


def touch_ends(entries, rng, smallest, high):
    longest = entries.shape.index(max(entries.shape))
    spots = []
    for shift in (0, 1):
        where = [jax.random.randint(jax.random.fold_in(rng, axis), (), 0, length) for axis, length in enumerate(entries.shape)]
        where[longest] = (where[longest] + shift) % entries.shape[longest]
        spots.append(tuple(where))
    return entries.at[spots[0]].set(smallest).at[spots[1]].set(high)


def levels(key, shape, cuts, least, top_value):
    def one(axis_at, shards_of):
        steps = jax.random.uniform(jax.random.fold_in(jax.random.fold_in(key, 6), axis_at), (shards_of,), jnp.float32, least / len(cuts), top_value / len(cuts))
        return jnp.repeat(jnp.exp(steps), shape[axis_at] // shards_of).reshape((-1,) + (1,) * (len(shape) - axis_at - 1))

    factor_of = one(*cuts[0])
    for cut in cuts[1:]:
        factor_of = factor_of * one(*cut)
    return factor_of


def gaussian(stream_key, dims, spread, bound, cuts=(), kind=jnp.bfloat16):
    drawn = jax.random.normal(stream_key, dims, jnp.float32) * spread
    if len(cuts) > 0:
        drawn = levels(stream_key, dims, cuts, -0.22, 0.18) * drawn
    return jnp.clip(drawn, min=-bound, max=bound).astype(kind)


def setup_inputs(seed: int = 0) -> dict:
    keys = jax.random.split(jax.random.key(seed), 12)
    observations = draw_observations(jax.random.fold_in(keys[11], 71), 0)
    counts = draw_counts(jax.random.fold_in(keys[11], 71), 0)
    visible = touch_ends((jax.random.randint(keys[2], (REGIONS, REGIONS), 0, 2) < 1).astype(jnp.int32), jax.random.fold_in(keys[2], 1), 0, 1)
    latents = gaussian(keys[3], (REGIONS, LR, D), 1.0, 6.0, ((0, 32),))
    lat_gain = jnp.clip(1.0 + 0.1 * jax.random.normal(keys[4], (D,), jnp.float32), 0.5, 1.5)
    mlp_gain = jnp.clip(1.0 + 0.1 * jax.random.normal(keys[5], (D,), jnp.float32), 0.5, 1.5)
    w_query = gaussian(keys[6], (D, D), D ** -0.5, 0.25)
    w_keyval = gaussian(keys[7], (D, 2 * D), D ** -0.5, 0.25)
    w_out = gaussian(keys[8], (D, D), D ** -0.5, 0.25)
    w_up = gaussian(keys[9], (D, HID), D ** -0.5, 0.25, ((1, 8),))
    w_down = gaussian(keys[10], (HID, D), HID ** -0.5, 0.125, ((0, 8),))
    return {"observations": observations, "counts": counts, "visible": visible, "latents": latents, "lat_gain": lat_gain, "mlp_gain": mlp_gain, "w_query": w_query, "w_keyval": w_keyval, "w_out": w_out, "w_up": w_up, "w_down": w_down}


NEG = -1e+30

def layer_norm(values, gain):
    average = lax.optimization_barrier(jnp.mean(values, axis=-1, keepdims=True))
    centered = values - average
    variance = lax.optimization_barrier(jnp.mean(centered * centered, axis=-1, keepdims=True))
    return centered * lax.rsqrt(variance + 1e-05) * gain

def expand(factor, model_width):
    return jnp.repeat(factor, model_width // factor.shape[-1], axis=-1)

def combine(first, second):
    first_num, first_den, first_peak = first
    second_num, second_den, second_peak = second
    highest = jnp.maximum(first_peak, second_peak)
    first_scale = jnp.exp(first_peak - highest)
    second_scale = jnp.exp(second_peak - highest)
    numerator = first_num * expand(first_scale, first_num.shape[-1]) + second_num * expand(second_scale, second_num.shape[-1])
    return (numerator, first_den * first_scale + second_den * second_scale, highest)

def partials(query_rows, key_rows, value_rows, allowed):
    row_count = query_rows.shape[0]
    key_count = key_rows.shape[0]
    query_heads = query_rows.astype(jnp.float32).reshape(row_count, H, DH)
    key_heads = key_rows.astype(jnp.float32).reshape(key_count, H, DH)
    value_heads = value_rows.astype(jnp.float32).reshape(key_count, H, DH)
    scores = jnp.einsum('qhd,khd->hqk', query_heads, key_heads) * DH ** (-0.5)
    scores = jnp.where(allowed[None], scores, NEG)
    peaks = lax.optimization_barrier(jnp.max(scores, axis=-1))
    weights = jnp.where(allowed[None], jnp.exp(scores - peaks[..., None]), 0.0)
    denominator = lax.optimization_barrier(jnp.sum(weights, axis=-1))
    rounded = weights.astype(jnp.bfloat16).astype(jnp.float32)
    numerator = jnp.einsum('hqk,khd->qhd', rounded, value_heads).reshape(row_count, H * DH)
    return (numerator, denominator.T, peaks.T)

def reference(observations, counts, visible, latents, lat_gain, mlp_gain, w_query, w_keyval, w_out, w_up, w_down):
    obs_rows = CAP * BLK

    def project(blocks):
        flat = blocks.reshape(SLOTS * obs_rows, D)
        return jnp.dot(flat, w_keyval, preferred_element_type=jnp.float32).astype(jnp.bfloat16).reshape(SLOTS, obs_rows, 2 * D)
    keyval = lax.map(project, observations)
    latent_rows = latents.astype(jnp.float32)
    normed = layer_norm(latent_rows, lat_gain).astype(jnp.bfloat16).reshape(REGIONS * LR, D)
    queries = jnp.dot(normed, w_query, preferred_element_type=jnp.float32).astype(jnp.bfloat16).reshape(REGIONS, LR, D)
    live_rows = jnp.arange(obs_rows, dtype=jnp.int32)[None, None, :] < counts[:, :, None] * BLK

    def per_latent(region_id):
        region_queries = queries[region_id]

        def step(carried, source_id):
            sees_source = (visible[region_id, source_id] > 0) | (region_id == source_id)

            def compute(unused):

                def per_slot(slot_id):
                    block = keyval[source_id, slot_id]
                    allowed = jnp.broadcast_to(live_rows[source_id, slot_id][None, :], (LR, obs_rows))
                    return partials(region_queries, block[:, :D], block[:, D:], allowed)
                nums, dens, peaks = lax.map(per_slot, jnp.arange(SLOTS, dtype=jnp.int32))
                result = (nums[0], dens[0], peaks[0])
                for slot_id in range(1, SLOTS):
                    result = combine(result, (nums[slot_id], dens[slot_id], peaks[slot_id]))
                return result

            def skipped(unused):
                return (jnp.zeros((LR, D), jnp.float32), jnp.zeros((LR, H), jnp.float32), jnp.full((LR, H), NEG, jnp.float32))
            piece_set = lax.cond(sees_source, compute, skipped, None)
            return (combine(carried, piece_set), None)
        initial = (jnp.zeros((LR, D), jnp.float32), jnp.zeros((LR, H), jnp.float32), jnp.full((LR, H), NEG, jnp.float32))
        final, unused = lax.scan(step, initial, jnp.arange(REGIONS, dtype=jnp.int32))
        return final[0] / expand(final[1], D)
    attended = lax.map(per_latent, jnp.arange(REGIONS, dtype=jnp.int32)).astype(jnp.bfloat16).reshape(REGIONS * LR, D)
    residual = latent_rows.reshape(REGIONS * LR, D) + jnp.dot(attended, w_out, preferred_element_type=jnp.float32)
    normed2 = layer_norm(residual, mlp_gain).astype(jnp.bfloat16)
    hidden = jax.nn.gelu(jnp.dot(normed2, w_up, preferred_element_type=jnp.float32), approximate=True).astype(jnp.bfloat16)
    encoded = residual + jnp.dot(hidden, w_down, preferred_element_type=jnp.float32)
    return encoded.astype(jnp.bfloat16).reshape(REGIONS, LR, D)
```

```python
import functools

import jax
import jax.numpy as jnp
from jax import lax
from jax.experimental import pallas as pl
from jax.experimental.pallas import tpu as pltpu
from jax.sharding import PartitionSpec as P

H = 8
BLK = 256
NZ, NX = 8, 4
EPS = 1e-05
NEG = -1e30
D = 512
DH = 64
LR = 32
WIDE = D + 128
BF = jnp.bfloat16
F32 = jnp.float32


def lanes_of(shape):
    return lax.broadcasted_iota(jnp.int32, shape, len(shape) - 1)


def norm_rows(values, gain):
    average = jnp.mean(values, axis=-1, keepdims=True)
    centered = values - average
    variance = jnp.mean(centered * centered, axis=-1, keepdims=True)
    return centered * lax.rsqrt(variance + EPS) * gain


def whole(shape):
    return pl.BlockSpec(shape, lambda *_: (0,) * len(shape))


def query_kernel(lat_ref, gain_ref, wq_ref, out_ref):
    normed = norm_rows(lat_ref[...].astype(F32), gain_ref[...]).astype(BF)
    q = jnp.dot(normed, wq_ref[...], preferred_element_type=F32).astype(BF)
    out_ref[...] = q * jnp.asarray(DH ** -0.5, BF)


def pack_stats(lse):
    lane = lanes_of(lse.shape)
    high = lse.astype(BF).astype(F32)
    rest = lse - high
    mid = rest.astype(BF).astype(F32)
    low = rest - mid
    kept = jnp.where(lane < 8, high, jnp.where(lane < 16, mid, jnp.where(lane < 24, low, 0.0)))
    return kept.astype(BF)


def attend_kernel(meta_ref, vis_ref, q_ref, kt_ref, va_ref, out_ref, list_ref, q_s):
    count = meta_ref[0]
    z, x, t, shift = meta_ref[1], meta_ref[2], meta_ref[3], meta_ref[4]
    own = z * NX + x
    first = lax.rem(t - 2 * shift + 8, 8)
    second = lax.rem(t - 2 * shift + 7, 8)
    column = lax.rem(x - shift + NX, NX)
    seen = jnp.int32(0)
    for e in range(NZ):
        region = lax.rem(z - e + NZ, NZ) * NX + column
        list_ref[seen] = jnp.int32(e)
        sees = (vis_ref[region] > 0) | (region == own)
        seen = seen + sees.astype(jnp.int32)
    last = list_ref[jnp.maximum(seen - 1, 0)]
    for k in range(3):
        list_ref[seen + k] = last

    lane = lanes_of((LR, 128))
    out_ref[:, :, :D] = jnp.zeros((NZ, LR, D), BF)
    out_ref[:, :, D:] = jnp.broadcast_to(
        jnp.where(lane < 8, NEG, 0.0).astype(BF)[None], (NZ, LR, 128)
    )

    def group(g, blocks):
        keys = blocks * BLK
        entries = [list_ref[4 * g + k] for k in range(4)]
        for k, e in enumerate(entries):
            q_s[pl.ds(32 * k, 16), :] = q_ref[first, e]
            q_s[pl.ds(32 * k + 16, 16), :] = q_ref[second, e]
        wide = lanes_of((128, 128))
        low_half = wide < DH
        odd_live = lax.rem(count, 2) == 0

        def pair(p, stats):
            here = pl.ds(pl.multiple_of(128 * p, 128), 128)
            even_at = pl.ds(pl.multiple_of(256 * p, 128), 128)
            odd_at = pl.ds(pl.multiple_of(256 * p + 128, 128), 128)
            qp = q_s[:, here]
            zero = jnp.zeros_like(qp)
            both = jnp.concatenate([jnp.where(low_half, qp, zero), jnp.where(low_half, zero, qp)], 0)
            scores = jnp.dot(both, kt_ref[here, :keys], preferred_element_type=F32)
            tail = jnp.where(odd_live, scores[:, keys - BLK :], NEG)
            scores = jnp.concatenate([scores[:, : keys - BLK], tail], 1)
            peak = jnp.max(scores, axis=-1, keepdims=True)
            weights = jnp.exp(scores - peak).astype(BF)
            even = jnp.dot(weights[:128], va_ref[:keys, even_at], preferred_element_type=F32)
            odd = jnp.dot(weights[128:], va_ref[:keys, odd_at], preferred_element_type=F32)
            total = pltpu.roll(jnp.where(low_half, odd, even), DH, 1)
            value = (jnp.where(low_half, even, odd) / total).astype(BF)
            lse = jnp.where(low_half, peak[:128], peak[128:]) + jnp.log(total)
            turned = pltpu.roll(lse, DH, 1)
            within = wide & 7
            stats = jnp.where(within == 2 * p, lse, jnp.where(within == 2 * p + 1, turned, stats))
            for k, e in enumerate(entries):
                out_ref[e, :, here] = value[32 * k : 32 * (k + 1)]
            return stats

        unroll = 2 if blocks == 8 else 1

        def pairs(i, stats):
            for k in range(unroll):
                stats = pair(i * unroll + k, stats)
            return stats

        stats = lax.fori_loop(0, H // 2 // unroll, pairs, jnp.zeros((128, 128), F32))
        packed = pack_stats(stats)
        for k, e in enumerate(entries):
            out_ref[e, :, D:] = packed[32 * k : 32 * (k + 1)]

    groups = (seen + 3) // 4
    for half in range(1, 5):

        @pl.when((count + 1) // 2 == half)
        def _():
            def body(g, carry):
                group(g, 2 * half)
                return carry

            lax.fori_loop(0, groups, body, 0)


def attend(meta, seen_by, queries, keys_t, values):
    return pl.pallas_call(
        attend_kernel,
        out_shape=jax.ShapeDtypeStruct((NZ, LR, WIDE), BF),
        in_specs=[
            pl.BlockSpec(memory_space=pltpu.SMEM),
            pl.BlockSpec(memory_space=pltpu.SMEM),
            pl.BlockSpec(memory_space=pltpu.VMEM),
            pl.BlockSpec(memory_space=pltpu.VMEM),
            pl.BlockSpec(memory_space=pltpu.VMEM),
        ],
        out_specs=pl.BlockSpec(memory_space=pltpu.VMEM),
        scratch_shapes=[pltpu.SMEM((16,), jnp.int32), pltpu.VMEM((128, D), BF)],
        compiler_params=pltpu.CompilerParams(vmem_limit_bytes=40 << 20),
        cost_estimate=pl.CostEstimate(flops=2 << 30, bytes_accessed=8 << 20, transcendentals=2 << 20),
        name="attend",
    )(meta, seen_by, queries, keys_t, values)


def spread_matrix():
    row = lax.broadcasted_iota(jnp.int32, (128, WIDE), 0)
    col = lax.broadcasted_iota(jnp.int32, (128, WIDE), 1)
    head = jnp.where(col < D, col // DH, jnp.where(col < D + 24, col & 7, -1))
    return jnp.where((row < 24) & ((row & 7) == head), 1.0, 0.0).astype(BF)


def join(pieces, spread):
    lses = [jnp.dot(p[:, D:], spread, preferred_element_type=F32) for p in pieces]
    highest = functools.reduce(jnp.maximum, lses)
    scales = [jnp.exp(l - highest) for l in lses]
    total = functools.reduce(jnp.add, scales)
    value = functools.reduce(
        jnp.add, [p[:, :D].astype(F32) * s[:, :D] for p, s in zip(pieces, scales)]
    )
    return value / total[:, :D], (highest + jnp.log(total))[:, D:]


def join_kernel(count, *refs):
    pieces = [r[...] for r in refs[:count]]
    outs = refs[count:]
    value, lse = join(pieces, spread_matrix())
    value, packed = value.astype(BF), pack_stats(lse)
    rows = value.shape[0] // len(outs)
    for k, out in enumerate(outs):
        out[:, :D] = value[rows * k : rows * (k + 1)]
        out[:, D:] = packed[rows * k : rows * (k + 1)]


def joined(pieces, outputs):
    rows = pieces[0].shape[0] // outputs
    return pl.pallas_call(
        functools.partial(join_kernel, len(pieces)),
        out_shape=[jax.ShapeDtypeStruct((rows, WIDE), BF)] * outputs,
        in_specs=[pl.BlockSpec(memory_space=pltpu.VMEM)] * len(pieces),
        out_specs=[pl.BlockSpec(memory_space=pltpu.VMEM)] * outputs,
        compiler_params=pltpu.CompilerParams(vmem_limit_bytes=16 << 20),
        name="join_pieces",
    )(*pieces)


def final_kernel(pieces_ref, lat_ref, gain_ref, wo_ref, up_ref, down_ref, out_ref):
    pieces = [pieces_ref[k] for k in range(8)]
    value, _ = join(pieces, spread_matrix())
    attended = value.astype(BF)
    residual = lat_ref[...].astype(F32) + jnp.dot(attended, wo_ref[...], preferred_element_type=F32)
    normed = norm_rows(residual, gain_ref[...]).astype(BF)
    total = residual
    for k in range(up_ref.shape[0]):
        v = jnp.dot(normed, up_ref[k], preferred_element_type=F32)
        hidden = jax.nn.gelu(v, approximate=True).astype(BF)
        total = total + jnp.dot(hidden, down_ref[k], preferred_element_type=F32)
    out_ref[...] = total.astype(BF)


def shifted_x(a, by):
    pairs = [
        (zz * NX + xx, zz * NX + (xx + by) % NX) for zz in range(NZ) for xx in range(NX)
    ]
    return lax.ppermute(a, "region", pairs) if by % NX else a


def shifted_z(a, by):
    pairs = [
        (zz * NX + xx, (zz + by) % NZ * NX + xx) for zz in range(NZ) for xx in range(NX)
    ]
    return lax.ppermute(a, "region", pairs) if by % NZ else a


def shifted_t(a, by):
    return lax.ppermute(a, "tm", [(k, (k + by) % 8) for k in range(8)]) if by % 8 else a


def on_device(
    observations,
    counts,
    visible,
    latents,
    lat_gain,
    mlp_gain,
    w_query,
    w_keyval,
    w_out,
    w_up,
    w_down,
):
    own = lax.axis_index("region")
    slot = lax.axis_index("tm")
    z, x = own // NX, own % NX
    observed = observations[0, 0]
    lat = latents[0]

    with jax.named_scope("queries"):
        q = pl.pallas_call(
            query_kernel, out_shape=jax.ShapeDtypeStruct((LR, D), BF), name="queries"
        )(lat, lat_gain[None], w_query)
    with jax.named_scope("gather_x"):
        near = jnp.concatenate([shifted_x(q, d) for d in range(NX)])
        part = lax.dynamic_slice_in_dim(near, slot * 16, 16, 0)
    with jax.named_scope("gather_z"):
        part = jnp.stack([shifted_z(part, e) for e in range(NZ)])
    with jax.named_scope("gather_t"):
        queries = jnp.stack([shifted_t(part, f) for f in range(8)])

    with jax.named_scope("keyval"):
        keys_t = lax.dot_general(
            w_keyval[:, :D], observed, (((0,), (1,)), ((), ())), preferred_element_type=F32
        ).astype(BF)
        wv = w_keyval[:, D:].reshape(D, H // 2, 2, DH)
        gap = jnp.zeros((D, H // 2, DH), BF)
        wide = jnp.concatenate([wv[:, :, 0], gap, gap, wv[:, :, 1]], -1).reshape(D, 2 * D)
        place = lax.iota(jnp.int32, 2 * D) % 256
        ones = jnp.where((place >= DH) & (place < 3 * DH), 1.0, 0.0)
        values = (jnp.dot(observed, wide, preferred_element_type=F32) + ones).astype(BF)

    with jax.named_scope("weights"):
        up = lax.all_gather(w_up, "tm")
        down = lax.all_gather(w_down, "tm")

    seen_by = lax.dynamic_slice_in_dim(visible, own, 1, 1)[:, 0]
    base = jnp.stack([counts[0, 0], z, x, slot]).astype(jnp.int32)
    with jax.named_scope("attend"):
        pieces = {}
        for d in (2, 1, 3, 0):
            meta = jnp.concatenate([base, jnp.array([d, 0, 0, 0], jnp.int32)])
            part = attend(meta, seen_by, queries, keys_t, values)
            pieces[d] = shifted_x(part.reshape(NZ * LR, WIDE), -d)
    with jax.named_scope("join_x"):
        parts = joined([pieces[d] for d in range(NX)], NZ)
    with jax.named_scope("join_z"):
        (part,) = joined([shifted_z(parts[e], -e) for e in range(NZ)], 1)
    with jax.named_scope("join_t"):
        pieces = lax.all_to_all(
            jnp.broadcast_to(part[None], (8, LR, WIDE)), "tm", 0, 0, tiled=True
        )
    with jax.named_scope("final"):
        out = pl.pallas_call(
            final_kernel,
            out_shape=jax.ShapeDtypeStruct((LR, D), BF),
            compiler_params=pltpu.CompilerParams(vmem_limit_bytes=24 << 20),
            name="final",
        )(pieces, lat, mlp_gain[None], w_out, up, down)
    return out[None]


def solution(mesh):
    placed = (
        P("region", "tm", None, None),
        P("region", "tm"),
        P(),
        P("region", None, None),
        P(),
        P(),
        P(),
        P(),
        P(),
        P(None, "tm"),
        P("tm", None),
    )
    return jax.shard_map(
        on_device, mesh=mesh, in_specs=placed, out_specs=P("region", None, None), check_vma=False
    )
```

```python
import functools

import jax
import jax.numpy as jnp
from jax import lax
from jax.experimental import pallas as pl
from jax.experimental.pallas import tpu as pltpu
from jax.sharding import PartitionSpec as P

H = 8
BLK = 256
NZ, NX = 8, 4
EPS = 1e-05
NEG = -1e30
D = 512
DH = 64
LR = 32
WIDE = D + 128
BF = jnp.bfloat16
F32 = jnp.float32


def lanes_of(shape):
    return lax.broadcasted_iota(jnp.int32, shape, len(shape) - 1)


def norm_rows(values, gain):
    average = jnp.mean(values, axis=-1, keepdims=True)
    centered = values - average
    variance = jnp.mean(centered * centered, axis=-1, keepdims=True)
    return centered * lax.rsqrt(variance + EPS) * gain


def whole(shape):
    return pl.BlockSpec(shape, lambda *_: (0,) * len(shape))


def query_kernel(half_ref, lat_ref, gain_ref, wq_ref, out_ref, q_s):
    normed = norm_rows(lat_ref[...].astype(F32), gain_ref[...]).astype(BF)
    q = jnp.dot(normed, wq_ref[...], preferred_element_type=F32).astype(BF)
    q_s[...] = q * jnp.asarray(DH ** -0.5, BF)
    rows = q_s[pl.ds(pl.multiple_of(half_ref[0] * 16, 16), 16), :]
    out_ref[...] = jnp.broadcast_to(rows[None], out_ref.shape)


def pack_stats(lse):
    lane = lanes_of(lse.shape)
    high = lse.astype(BF).astype(F32)
    rest = lse - high
    mid = rest.astype(BF).astype(F32)
    low = rest - mid
    kept = jnp.where(lane < 8, high, jnp.where(lane < 16, mid, jnp.where(lane < 24, low, 0.0)))
    return kept.astype(BF)


def attend_kernel(meta_ref, vis_ref, near_ref, far_ref, kt_ref, va_ref, out_ref, list_ref, q_s):
    count = meta_ref[0]
    own, core, column = meta_ref[1], meta_ref[2], meta_ref[3]
    seen = jnp.int32(0)
    for e in range(NZ):
        region = e * NX + column
        list_ref[seen] = jnp.int32(e)
        sees = (vis_ref[region] > 0) | (region == own)
        seen = seen + sees.astype(jnp.int32)
    last = list_ref[jnp.maximum(seen - 1, 0)]
    for k in range(3):
        list_ref[seen + k] = last

    lane = lanes_of((LR, 128))
    out_ref[:, :, :D] = jnp.zeros((NZ, LR, D), BF)
    out_ref[:, :, D:] = jnp.broadcast_to(
        jnp.where(lane < 8, NEG, 0.0).astype(BF)[None], (NZ, LR, 128)
    )

    def group(g, blocks):
        keys = blocks * BLK
        entries = [list_ref[4 * g + k] for k in range(4)]
        for k, e in enumerate(entries):
            region = e * NX + column
            q_s[pl.ds(pl.multiple_of(32 * k + 16 * core, 16), 16), :] = near_ref[region]
            q_s[pl.ds(pl.multiple_of(32 * k + 16 - 16 * core, 16), 16), :] = far_ref[region]
        wide = lanes_of((128, 128))
        low_half = wide < DH
        odd_live = lax.rem(count, 2) == 0

        def pair(p, stats):
            here = pl.ds(pl.multiple_of(128 * p, 128), 128)
            even_at = pl.ds(pl.multiple_of(256 * p, 128), 128)
            odd_at = pl.ds(pl.multiple_of(256 * p + 128, 128), 128)
            qp = q_s[:, here]
            zero = jnp.zeros_like(qp)
            both = jnp.concatenate([jnp.where(low_half, qp, zero), jnp.where(low_half, zero, qp)], 0)
            scores = jnp.dot(both, kt_ref[here, :keys], preferred_element_type=F32)
            tail = jnp.where(odd_live, scores[:, keys - BLK :], NEG)
            scores = jnp.concatenate([scores[:, : keys - BLK], tail], 1)
            peak = jnp.max(scores, axis=-1, keepdims=True)
            weights = jnp.exp(scores - peak).astype(BF)
            even = jnp.dot(weights[:128], va_ref[:keys, even_at], preferred_element_type=F32)
            odd = jnp.dot(weights[128:], va_ref[:keys, odd_at], preferred_element_type=F32)
            total = pltpu.roll(jnp.where(low_half, odd, even), DH, 1)
            value = (jnp.where(low_half, even, odd) / total).astype(BF)
            lse = jnp.where(low_half, peak[:128], peak[128:]) + jnp.log(total)
            turned = pltpu.roll(lse, DH, 1)
            within = wide & 7
            stats = jnp.where(within == 2 * p, lse, jnp.where(within == 2 * p + 1, turned, stats))
            for k, e in enumerate(entries):
                out_ref[e, :, here] = value[32 * k : 32 * (k + 1)]
            return stats

        unroll = 2 if blocks == 8 else 1

        def pairs(i, stats):
            for k in range(unroll):
                stats = pair(i * unroll + k, stats)
            return stats

        stats = lax.fori_loop(0, H // 2 // unroll, pairs, jnp.zeros((128, 128), F32))
        packed = pack_stats(stats)
        for k, e in enumerate(entries):
            out_ref[e, :, D:] = packed[32 * k : 32 * (k + 1)]

    groups = (seen + 3) // 4
    for half in range(1, 5):

        @pl.when((count + 1) // 2 == half)
        def _():
            def body(g, carry):
                group(g, 2 * half)
                return carry

            lax.fori_loop(0, groups, body, 0)


def attend(meta, seen_by, near, far, keys_t, values):
    scalars = pl.BlockSpec(memory_space=pltpu.SMEM)
    vectors = pl.BlockSpec(memory_space=pltpu.VMEM)
    return pl.pallas_call(
        attend_kernel,
        out_shape=jax.ShapeDtypeStruct((NZ, LR, WIDE), BF),
        in_specs=[scalars] * 2 + [vectors] * 4,
        out_specs=vectors,
        scratch_shapes=[pltpu.SMEM((16,), jnp.int32), pltpu.VMEM((128, D), BF)],
        compiler_params=pltpu.CompilerParams(vmem_limit_bytes=20 << 20),
        cost_estimate=pl.CostEstimate(flops=2 << 30, bytes_accessed=8 << 20, transcendentals=2 << 20),
        name="attend",
    )(meta, seen_by, near, far, keys_t, values)


def spread_matrix():
    row = lax.broadcasted_iota(jnp.int32, (128, WIDE), 0)
    col = lax.broadcasted_iota(jnp.int32, (128, WIDE), 1)
    head = jnp.where(col < D, col // DH, jnp.where(col < D + 24, col & 7, -1))
    return jnp.where((row < 24) & ((row & 7) == head), 1.0, 0.0).astype(BF)


def join(pieces, spread):
    lses = [jnp.dot(p[:, D:], spread, preferred_element_type=F32) for p in pieces]
    highest = functools.reduce(jnp.maximum, lses)
    scales = [jnp.exp(l - highest) for l in lses]
    total = functools.reduce(jnp.add, scales)
    value = functools.reduce(
        jnp.add, [p[:, :D].astype(F32) * s[:, :D] for p, s in zip(pieces, scales)]
    )
    return value / total[:, :D], (highest + jnp.log(total))[:, D:]


def join_kernel(*refs):
    *ins, out = refs
    pieces = [r[...] for r in ins] if len(ins) > 1 else [ins[0][k] for k in range(ins[0].shape[0])]
    value, lse = join(pieces, spread_matrix())
    out[..., :D] = jnp.broadcast_to(value.astype(BF), (*out.shape[:-1], D))
    out[..., D:] = jnp.broadcast_to(pack_stats(lse), (*out.shape[:-1], 128))


def joined(pieces, shape):
    return pl.pallas_call(
        join_kernel,
        out_shape=jax.ShapeDtypeStruct(shape, BF),
        in_specs=[pl.BlockSpec(memory_space=pltpu.VMEM)] * len(pieces),
        out_specs=pl.BlockSpec(memory_space=pltpu.VMEM),
        compiler_params=pltpu.CompilerParams(vmem_limit_bytes=16 << 20),
        name="join_pieces",
    )(*pieces)


def final_kernel(row_ref, pieces_ref, lat_ref, gain_ref, wo_ref, *refs):
    weights, (res_ref, part_ref, sums) = refs[:4], refs[4:]
    pieces = [pieces_ref[k] for k in range(8)]
    value, _ = join(pieces, spread_matrix())
    attended = value.astype(BF)
    residual = lat_ref[...].astype(F32) + jnp.dot(attended, wo_ref[...], preferred_element_type=F32)
    normed = norm_rows(residual, gain_ref[...]).astype(BF)
    res_ref[...] = residual
    for k, w in enumerate(weights):
        v = jnp.dot(normed, w[:, :256], preferred_element_type=F32)
        hidden = jax.nn.gelu(v, approximate=True).astype(BF)
        down = jnp.concatenate([w[:256, 256:], w[256:, 256:]], 1)
        sums[lax.rem(row_ref[0] - k + 4, 4)] = jnp.dot(hidden, down, preferred_element_type=F32)
    part_ref[...] = (sums[0] + sums[1]) + (sums[2] + sums[3])


def shifted_x(a, by):
    pairs = [
        (zz * NX + xx, zz * NX + (xx + by) % NX) for zz in range(NZ) for xx in range(NX)
    ]
    return lax.ppermute(a, "region", pairs) if by % NX else a


def shifted_y(a, by):
    return lax.ppermute(a, "tm", [(k, (k + 2 * by) % 8) for k in range(8)]) if by % 4 else a


def core_swapped(a):
    return lax.ppermute(a, "tm", [(k, k ^ 1) for k in range(8)])


def on_device(
    observations,
    counts,
    visible,
    latents,
    lat_gain,
    mlp_gain,
    w_query,
    w_keyval,
    w_out,
    w_up,
    w_down,
):
    own = lax.axis_index("region")
    slot = lax.axis_index("tm")
    x, row, core = own % NX, slot // 2, slot % 2
    observed = observations[0, 0]
    lat = latents[0]
    scalars = pl.BlockSpec(memory_space=pltpu.SMEM)
    vectors = pl.BlockSpec(memory_space=pltpu.VMEM)

    with jax.named_scope("queries"):
        q = pl.pallas_call(
            query_kernel,
            out_shape=jax.ShapeDtypeStruct((NZ * NX, 16, D), BF),
            in_specs=[scalars] + [vectors] * 3,
            out_specs=vectors,
            scratch_shapes=[pltpu.VMEM((LR, D), BF)],
            name="queries",
        )(core[None], lat, lat_gain[None], w_query)
    with jax.named_scope("gather"):
        near = lax.all_to_all(q, "region", 0, 0, tiled=True)
        far = core_swapped(near)

    with jax.named_scope("weights"):
        mlp = jnp.concatenate([w_up, jnp.concatenate([w_down[:, :256], w_down[:, 256:]], 0)], 1)
        shards = [shifted_y(mlp, k) for k in range(4)]

    with jax.named_scope("keyval"):
        keys_t = lax.dot_general(
            w_keyval[:, :D], observed, (((0,), (1,)), ((), ())), preferred_element_type=F32
        ).astype(BF)
        wv = w_keyval[:, D:].reshape(D, H // 2, 2, DH)
        gap = jnp.zeros((D, H // 2, DH), BF)
        wide = jnp.concatenate([wv[:, :, 0], gap, gap, wv[:, :, 1]], -1).reshape(D, 2 * D)
        place = lax.iota(jnp.int32, 2 * D) % 256
        ones = jnp.where((place >= DH) & (place < 3 * DH), 1.0, 0.0)
        values = (jnp.dot(observed, wide, preferred_element_type=F32) + ones).astype(BF)

    seen_by = lax.dynamic_slice_in_dim(visible, own, 1, 1)[:, 0]
    with jax.named_scope("attend"):
        pieces = []
        for d in (2, 1, 3, 0):
            meta = jnp.stack([counts[0, 0], own, core, (x - d) % NX]).astype(jnp.int32)
            if d == 0:
                meta, *shards = lax.optimization_barrier((meta, *shards))
            part = attend(meta, seen_by, near, far, keys_t, values)
            pieces.append(shifted_x(part.reshape(NZ * LR, WIDE), -d))
    with jax.named_scope("join_x"):
        part = joined(pieces, (NZ * LR, WIDE)).reshape(NZ, LR, WIDE)
    with jax.named_scope("join_z"):
        groups = [[zz * NX + xx for zz in range(NZ)] for xx in range(NX)]
        part = lax.all_to_all(part, "region", 0, 0, axis_index_groups=groups, tiled=True)
        part = joined([part], (8, LR, WIDE))
    with jax.named_scope("join_t"):
        pieces = lax.all_to_all(part, "tm", 0, 0, tiled=True)
    with jax.named_scope("final"):
        residual, mine = pl.pallas_call(
            final_kernel,
            out_shape=[jax.ShapeDtypeStruct((LR, D), F32)] * 2,
            in_specs=[scalars] + [vectors] * 8,
            out_specs=[vectors] * 2,
            scratch_shapes=[pltpu.VMEM((4, LR, D), F32)],
            compiler_params=pltpu.CompilerParams(vmem_limit_bytes=16 << 20),
            name="final",
        )(row[None], pieces, lat, mlp_gain[None], w_out, *shards)
        out = residual + (mine + core_swapped(mine))
    return out.astype(BF)[None]


def solution(mesh):
    placed = (
        P("region", "tm", None, None),
        P("region", "tm"),
        P(),
        P("region", None, None),
        P(),
        P(),
        P(),
        P(),
        P(),
        P(None, "tm"),
        P("tm", None),
    )
    return jax.shard_map(
        on_device, mesh=mesh, in_specs=placed, out_specs=P("region", None, None), check_vma=False
    )
```

```python
import functools

import jax
import jax.numpy as jnp
from jax import lax
from jax.experimental import pallas as pl
from jax.experimental.pallas import tpu as pltpu
from jax.sharding import PartitionSpec as P

H = 8
BLK = 256
NZ, NX = 8, 4
EPS = 1e-05
NEG = -1e30
D = 512
DH = 64
LR = 32
WIDE = D + 128
BF = jnp.bfloat16
F32 = jnp.float32


def lanes_of(shape):
    return lax.broadcasted_iota(jnp.int32, shape, len(shape) - 1)


def norm_rows(values, gain):
    average = jnp.mean(values, axis=-1, keepdims=True)
    centered = values - average
    variance = jnp.mean(centered * centered, axis=-1, keepdims=True)
    return centered * lax.rsqrt(variance + EPS) * gain


def whole(shape):
    return pl.BlockSpec(shape, lambda *_: (0,) * len(shape))


def query_kernel(half_ref, lat_ref, gain_ref, wq_ref, out_ref, q_s):
    normed = norm_rows(lat_ref[...].astype(F32), gain_ref[...]).astype(BF)
    q = jnp.dot(normed, wq_ref[...], preferred_element_type=F32).astype(BF)
    q_s[...] = q * jnp.asarray(DH ** -0.5, BF)
    rows = q_s[pl.ds(pl.multiple_of(half_ref[0] * 16, 16), 16), :]
    out_ref[...] = jnp.broadcast_to(rows[None], out_ref.shape)


def keyval_kernel(obs_ref, w_ref, up_ref, down_ref, k_ref, va_ref, mlp_ref):
    @pl.when(pl.program_id(0) == 0)
    def _():
        mlp_ref[:, :256] = up_ref[...]
        mlp_ref[:256, 256:] = down_ref[:, :256]
        mlp_ref[256:, 256:] = down_ref[:, 256:]

    kv = jnp.dot(obs_ref[...], w_ref[...], preferred_element_type=F32).astype(BF)
    k_ref[...] = kv[:, :D]
    low_half = lanes_of((kv.shape[0], 128)) < DH
    ones = jnp.ones((kv.shape[0], 128), BF)
    for p in range(H // 2):
        v = kv[:, D + 128 * p : D + 128 * (p + 1)]
        va_ref[:, 256 * p : 256 * p + 128] = jnp.where(low_half, v, ones)
        va_ref[:, 256 * p + 128 : 256 * p + 256] = jnp.where(low_half, ones, v)


def pack_stats(lse):
    lane = lanes_of(lse.shape)
    high = lse.astype(BF).astype(F32)
    rest = lse - high
    mid = rest.astype(BF).astype(F32)
    low = rest - mid
    kept = jnp.where(lane < 8, high, jnp.where(lane < 16, mid, jnp.where(lane < 24, low, 0.0)))
    return kept.astype(BF)


def attend_kernel(meta_ref, vis_ref, near_ref, far_ref, k_ref, va_ref, out_ref, list_ref, q_s):
    count = meta_ref[0]
    own, core, column = meta_ref[1], meta_ref[2], meta_ref[3]
    seen = jnp.int32(0)
    for e in range(NZ):
        region = e * NX + column
        list_ref[seen] = jnp.int32(e)
        sees = (vis_ref[region] > 0) | (region == own)
        seen = seen + sees.astype(jnp.int32)
    last = list_ref[jnp.maximum(seen - 1, 0)]
    for k in range(3):
        list_ref[seen + k] = last

    lane = lanes_of((LR, 128))
    out_ref[:, :, :D] = jnp.zeros((NZ, LR, D), BF)
    out_ref[:, :, D:] = jnp.broadcast_to(
        jnp.where(lane < 8, NEG, 0.0).astype(BF)[None], (NZ, LR, 128)
    )

    def group(start, regions, blocks, unroll):
        keys, rows = blocks * BLK, regions * LR
        entries = [list_ref[start + k] for k in range(regions)]
        for k, e in enumerate(entries):
            region = e * NX + column
            q_s[pl.ds(pl.multiple_of(32 * k + 16 * core, 16), 16), :] = near_ref[region]
            q_s[pl.ds(pl.multiple_of(32 * k + 16 - 16 * core, 16), 16), :] = far_ref[region]
        wide = lanes_of((rows, 128))
        low_half = wide < DH
        sure = max(1, blocks // 2 + (blocks > 2))

        def pair(p, stats):
            here = pl.ds(pl.multiple_of(128 * p, 128), 128)
            even_at = pl.ds(pl.multiple_of(256 * p, 128), 128)
            odd_at = pl.ds(pl.multiple_of(256 * p + 128, 128), 128)
            qp = q_s[:rows, here]
            zero = jnp.zeros_like(qp)
            both = jnp.concatenate([jnp.where(low_half, qp, zero), jnp.where(low_half, zero, qp)], 0)
            scores = lax.dot_general(
                both, k_ref[:keys, here], (((1,), (1,)), ((), ())), preferred_element_type=F32
            )
            parts = [scores[:, : sure * BLK]]
            for j in range(sure, blocks):
                parts.append(jnp.where(count > j, scores[:, j * BLK : (j + 1) * BLK], NEG))
            scores = jnp.concatenate(parts, 1)
            peak = jnp.max(scores, axis=-1, keepdims=True)
            weights = jnp.exp(scores - peak).astype(BF)
            even = jnp.dot(weights[:rows], va_ref[:keys, even_at], preferred_element_type=F32)
            odd = jnp.dot(weights[rows:], va_ref[:keys, odd_at], preferred_element_type=F32)
            total = pltpu.roll(jnp.where(low_half, odd, even), DH, 1)
            value = (jnp.where(low_half, even, odd) / total).astype(BF)
            lse = jnp.where(low_half, peak[:rows], peak[rows:]) + jnp.log(total)
            turned = pltpu.roll(lse, DH, 1)
            within = wide & 7
            stats = jnp.where(within == 2 * p, lse, jnp.where(within == 2 * p + 1, turned, stats))
            for k, e in enumerate(entries):
                out_ref[e, :, here] = value[32 * k : 32 * (k + 1)]
            return stats

        def pairs(i, stats):
            for k in range(unroll):
                stats = pair(i * unroll + k, stats)
            return stats

        stats = lax.fori_loop(0, H // 2 // unroll, pairs, jnp.zeros((rows, 128), F32))
        packed = pack_stats(stats)
        for k, e in enumerate(entries):
            out_ref[e, :, D:] = packed[32 * k : 32 * (k + 1)]

    for least, blocks in ((1, 2), (3, 4)):

        @pl.when((count >= least) & (count <= blocks))
        def _():
            def body(g, carry):
                group(4 * g, 4, blocks, 1)
                return carry

            lax.fori_loop(0, (seen + 3) // 4, body, 0)

    for fewest, regions, unroll in ((1, 4, 1), (5, 6, 2), (7, 8, 1)):

        @pl.when((count > 4) & (seen >= fewest) & (seen <= regions))
        def _():
            group(0, regions, 8, unroll)


def attend(meta, seen_by, near, far, keys, values):
    scalars = pl.BlockSpec(memory_space=pltpu.SMEM)
    vectors = pl.BlockSpec(memory_space=pltpu.VMEM)
    return pl.pallas_call(
        attend_kernel,
        out_shape=jax.ShapeDtypeStruct((NZ, LR, WIDE), BF),
        in_specs=[scalars] * 2 + [vectors] * 4,
        out_specs=vectors,
        scratch_shapes=[pltpu.SMEM((16,), jnp.int32), pltpu.VMEM((256, D), BF)],
        compiler_params=pltpu.CompilerParams(vmem_limit_bytes=24 << 20),
        cost_estimate=pl.CostEstimate(flops=2 << 30, bytes_accessed=8 << 20, transcendentals=2 << 20),
        name="attend",
    )(meta, seen_by, near, far, keys, values)


def spread_matrix():
    row = lax.broadcasted_iota(jnp.int32, (128, WIDE), 0)
    col = lax.broadcasted_iota(jnp.int32, (128, WIDE), 1)
    head = jnp.where(col < D, col // DH, jnp.where(col < D + 24, col & 7, -1))
    return jnp.where((row < 24) & ((row & 7) == head), 1.0, 0.0).astype(BF)


def join(pieces, spread):
    lses = [jnp.dot(p[:, D:], spread, preferred_element_type=F32) for p in pieces]
    highest = functools.reduce(jnp.maximum, lses)
    scales = [jnp.exp(l - highest) for l in lses]
    total = functools.reduce(jnp.add, scales)
    value = functools.reduce(
        jnp.add, [p[:, :D].astype(F32) * s[:, :D] for p, s in zip(pieces, scales)]
    )
    return value / total[:, :D], (highest + jnp.log(total))[:, D:]


def join_kernel(*refs):
    *ins, out = refs
    pieces = [r[...] for r in ins] if len(ins) > 1 else [ins[0][k] for k in range(ins[0].shape[0])]
    value, lse = join(pieces, spread_matrix())
    out[..., :D] = jnp.broadcast_to(value.astype(BF), (*out.shape[:-1], D))
    out[..., D:] = jnp.broadcast_to(pack_stats(lse), (*out.shape[:-1], 128))


def joined(pieces, shape):
    return pl.pallas_call(
        join_kernel,
        out_shape=jax.ShapeDtypeStruct(shape, BF),
        in_specs=[pl.BlockSpec(memory_space=pltpu.VMEM)] * len(pieces),
        out_specs=pl.BlockSpec(memory_space=pltpu.VMEM),
        compiler_params=pltpu.CompilerParams(vmem_limit_bytes=16 << 20),
        name="join_pieces",
    )(*pieces)


def final_kernel(row_ref, pieces_ref, lat_ref, gain_ref, wo_ref, *refs):
    weights, (res_ref, part_ref, sums) = refs[:4], refs[4:]
    pieces = [pieces_ref[k] for k in range(8)]
    value, _ = join(pieces, spread_matrix())
    attended = value.astype(BF)
    residual = lat_ref[...].astype(F32) + jnp.dot(attended, wo_ref[...], preferred_element_type=F32)
    normed = norm_rows(residual, gain_ref[...]).astype(BF)
    res_ref[...] = residual
    for k, w in enumerate(weights):
        v = jnp.dot(normed, w[:, :256], preferred_element_type=F32)
        hidden = jax.nn.gelu(v, approximate=True).astype(BF)
        down = jnp.concatenate([w[:256, 256:], w[256:, 256:]], 1)
        sums[lax.rem(row_ref[0] - k + 4, 4)] = jnp.dot(hidden, down, preferred_element_type=F32)
    part_ref[...] = (sums[0] + sums[1]) + (sums[2] + sums[3])


def shifted_x(a, by):
    pairs = [
        (zz * NX + xx, zz * NX + (xx + by) % NX) for zz in range(NZ) for xx in range(NX)
    ]
    return lax.ppermute(a, "region", pairs) if by % NX else a


def shifted_y(a, by):
    return lax.ppermute(a, "tm", [(k, (k + 2 * by) % 8) for k in range(8)]) if by % 4 else a


def core_swapped(a):
    return lax.ppermute(a, "tm", [(k, k ^ 1) for k in range(8)])


def on_device(
    observations,
    counts,
    visible,
    latents,
    lat_gain,
    mlp_gain,
    w_query,
    w_keyval,
    w_out,
    w_up,
    w_down,
):
    own = lax.axis_index("region")
    slot = lax.axis_index("tm")
    x, row, core = own % NX, slot // 2, slot % 2
    observed = observations[0, 0]
    lat = latents[0]
    scalars = pl.BlockSpec(memory_space=pltpu.SMEM)
    vectors = pl.BlockSpec(memory_space=pltpu.VMEM)

    with jax.named_scope("queries"):
        q = pl.pallas_call(
            query_kernel,
            out_shape=jax.ShapeDtypeStruct((NZ * NX, 16, D), BF),
            in_specs=[scalars] + [vectors] * 3,
            out_specs=vectors,
            scratch_shapes=[pltpu.VMEM((LR, D), BF)],
            name="queries",
        )(core[None], lat, lat_gain[None], w_query)
    with jax.named_scope("gather"):
        near = lax.all_to_all(q, "region", 0, 0, tiled=True)

    with jax.named_scope("keyval"):
        keys, values, mlp = pl.pallas_call(
            keyval_kernel,
            grid=(observed.shape[0] // BLK,),
            out_shape=[
                jax.ShapeDtypeStruct((observed.shape[0], D), BF),
                jax.ShapeDtypeStruct((observed.shape[0], 2 * D), BF),
                jax.ShapeDtypeStruct((D, D), BF),
            ],
            in_specs=[
                pl.BlockSpec((BLK, D), lambda i: (i, 0)),
                pl.BlockSpec((D, 2 * D), lambda i: (0, 0)),
                pl.BlockSpec((D, 256), lambda i: (0, 0)),
                pl.BlockSpec((256, D), lambda i: (0, 0)),
            ],
            out_specs=[
                pl.BlockSpec((BLK, D), lambda i: (i, 0)),
                pl.BlockSpec((BLK, 2 * D), lambda i: (i, 0)),
                pl.BlockSpec((D, D), lambda i: (0, 0)),
            ],
            compiler_params=pltpu.CompilerParams(vmem_limit_bytes=16 << 20),
            cost_estimate=pl.CostEstimate(flops=2 << 30, bytes_accessed=9 << 20, transcendentals=0),
            name="keyval",
        )(observed, w_keyval, w_up, w_down)

    near, values = lax.optimization_barrier((near, values))
    with jax.named_scope("gather"):
        far = core_swapped(near)
    with jax.named_scope("weights"):
        shards = [shifted_y(mlp, k) for k in range(4)]

    seen_by = lax.dynamic_slice_in_dim(visible, own, 1, 1)[:, 0]
    with jax.named_scope("attend"):
        pieces = []
        for d in (2, 1, 3, 0):
            meta = jnp.stack([counts[0, 0], own, core, (x - d) % NX]).astype(jnp.int32)
            if d == 0:
                meta, *shards = lax.optimization_barrier((meta, *shards))
            part = attend(meta, seen_by, near, far, keys, values)
            pieces.append(shifted_x(part.reshape(NZ * LR, WIDE), -d))
    with jax.named_scope("join_x"):
        part = joined(pieces, (NZ * LR, WIDE)).reshape(NZ, LR, WIDE)
    with jax.named_scope("join_z"):
        groups = [[zz * NX + xx for zz in range(NZ)] for xx in range(NX)]
        part = lax.all_to_all(part, "region", 0, 0, axis_index_groups=groups, tiled=True)
        part = joined([part], (8, LR, WIDE))
    with jax.named_scope("join_t"):
        pieces = lax.all_to_all(part, "tm", 0, 0, tiled=True)
    with jax.named_scope("final"):
        residual, mine = pl.pallas_call(
            final_kernel,
            out_shape=[jax.ShapeDtypeStruct((LR, D), F32)] * 2,
            in_specs=[scalars] + [vectors] * 8,
            out_specs=[vectors] * 2,
            scratch_shapes=[pltpu.VMEM((4, LR, D), F32)],
            compiler_params=pltpu.CompilerParams(vmem_limit_bytes=16 << 20),
            name="final",
        )(row[None], pieces, lat, mlp_gain[None], w_out, *shards)
        out = residual + (mine + core_swapped(mine))
    return out.astype(BF)[None]


def solution(mesh):
    placed = (
        P("region", "tm", None, None),
        P("region", "tm"),
        P(),
        P("region", None, None),
        P(),
        P(),
        P(),
        P(),
        P(),
        P(None, "tm"),
        P("tm", None),
    )
    return jax.shard_map(
        on_device, mesh=mesh, in_specs=placed, out_specs=P("region", None, None), check_vma=False
    )
```

```python
import functools

import jax
import jax.numpy as jnp
from jax import lax
from jax.experimental import pallas as pl
from jax.experimental.pallas import tpu as pltpu
from jax.sharding import PartitionSpec as P

H = 8
BLK = 256
NZ, NX = 8, 4
EPS = 1e-05
NEG = -1e30
D = 512
DH = 64
LR = 32
WIDE = D + 128
HALF = LR // 2
ROOM = 28 << 20
BF = jnp.bfloat16
F32 = jnp.float32


def lanes_of(shape):
    return lax.broadcasted_iota(jnp.int32, shape, len(shape) - 1)


def norm_rows(values, gain):
    average = jnp.mean(values, axis=-1, keepdims=True)
    centered = values - average
    variance = jnp.mean(centered * centered, axis=-1, keepdims=True)
    return centered * lax.rsqrt(variance + EPS) * gain


def whole(shape):
    return pl.BlockSpec(shape, lambda *_: (0,) * len(shape))


def query_kernel(half_ref, lat_ref, gain_ref, wq_ref, out_ref, q_s):
    normed = norm_rows(lat_ref[...].astype(F32), gain_ref[...]).astype(BF)
    q = jnp.dot(normed, wq_ref[...], preferred_element_type=F32).astype(BF)
    q_s[...] = q * jnp.asarray(DH ** -0.5, BF)
    rows = q_s[pl.ds(pl.multiple_of(half_ref[0] * 16, 16), 16), :]
    out_ref[...] = jnp.broadcast_to(rows[None], out_ref.shape)


def keyval_kernel(mine_ref, other_ref, w_ref, up_ref, down_ref, k_ref, va_ref, mlp_ref):
    @pl.when(pl.program_id(0) == 0)
    def _():
        mlp_ref[:, :256] = up_ref[...]
        mlp_ref[:256, 256:] = down_ref[:, :256]
        mlp_ref[256:, 256:] = down_ref[:, 256:]

    low_half = lanes_of((BLK, 128)) < DH
    ones = jnp.ones((BLK, 128), BF)
    for slot, obs_ref in enumerate((mine_ref, other_ref)):
        kv = jnp.dot(obs_ref[...], w_ref[...], preferred_element_type=F32).astype(BF)
        k_ref[slot] = kv[:, :D]
        for p in range(H // 2):
            v = kv[:, D + 128 * p : D + 128 * (p + 1)]
            va_ref[slot, :, 256 * p : 256 * p + 128] = jnp.where(low_half, v, ones)
            va_ref[slot, :, 256 * p + 128 : 256 * p + 256] = jnp.where(low_half, ones, v)


def pack_stats(lse):
    lane = lanes_of(lse.shape)
    high = lse.astype(BF).astype(F32)
    rest = lse - high
    mid = rest.astype(BF).astype(F32)
    low = rest - mid
    kept = jnp.where(lane < 8, high, jnp.where(lane < 16, mid, jnp.where(lane < 24, low, 0.0)))
    return kept.astype(BF)


def attend_kernel(shifts, meta_ref, vis_ref, near_ref, k_ref, va_ref, *rest):
    outs = rest[: len(shifts)]
    list_ref, q_s, v_s, l_s, out_s = rest[len(shifts) :]
    own, x = meta_ref[2], meta_ref[3]
    limit = NZ * len(shifts)
    columns = [lax.rem(x - d + NX, NX) for d in shifts]
    seen = jnp.int32(0)
    for j, column in enumerate(columns):
        for e in range(NZ):
            region = e * NX + column
            list_ref[0, seen] = region
            list_ref[1, seen] = jnp.int32(j * NZ + e)
            sees = (vis_ref[region] > 0) | (region == own)
            seen = seen + sees.astype(jnp.int32)
    last = jnp.maximum(seen - 1, 0)
    for k in range(7):
        for row in range(2):
            list_ref[row, seen + k] = list_ref[row, last]

    lane = lanes_of((HALF, 128))
    out_s[:, :, :D] = jnp.zeros((limit, HALF, D), BF)
    out_s[:, :, D:] = jnp.broadcast_to(
        jnp.where(lane < 8, NEG, 0.0).astype(BF)[None], (limit, HALF, 128)
    )

    def attend_slot(slot, count, rows, blocks, sure):
        keys = blocks * BLK
        low_half = lanes_of((rows, 128)) < DH

        def pair(p, carry):
            here = pl.ds(pl.multiple_of(128 * p, 128), 128)
            even_at = pl.ds(pl.multiple_of(256 * p, 128), 128)
            odd_at = pl.ds(pl.multiple_of(256 * p + 128, 128), 128)
            qp = q_s[:rows, here]
            zero = jnp.zeros_like(qp)
            both = jnp.concatenate([jnp.where(low_half, qp, zero), jnp.where(low_half, zero, qp)], 0)
            scores = lax.dot_general(
                both, k_ref[slot, :keys, here], (((1,), (1,)), ((), ())), preferred_element_type=F32
            )
            parts = [scores[:, : sure * BLK]]
            for j in range(sure, blocks):
                parts.append(jnp.where(count > j, scores[:, j * BLK : (j + 1) * BLK], NEG))
            scores = jnp.concatenate(parts, 1)
            peak = jnp.max(scores, axis=-1, keepdims=True)
            weights = jnp.exp(scores - peak).astype(BF)
            even = jnp.dot(weights[:rows], va_ref[slot, :keys, even_at], preferred_element_type=F32)
            odd = jnp.dot(weights[rows:], va_ref[slot, :keys, odd_at], preferred_element_type=F32)
            total = pltpu.roll(jnp.where(low_half, odd, even), DH, 1)
            value = jnp.where(low_half, even, odd) / total
            lse = jnp.where(low_half, peak[:rows], peak[rows:]) + jnp.log(total)
            before = l_s[:rows, here]
            highest = jnp.maximum(before, lse)
            old, new = jnp.exp(before - highest), jnp.exp(lse - highest)
            v_s[:rows, here] = (v_s[:rows, here] * old + value * new) / (old + new)
            l_s[:rows, here] = highest + jnp.log(old + new)
            return carry

        lax.fori_loop(0, H // 2, pair, 0)

    def run(regions):
        rows = regions * HALF
        for k in range(regions):
            q_s[HALF * k : HALF * (k + 1), :] = near_ref[list_ref[0, k]]
        v_s[:rows, :] = jnp.zeros((rows, D), F32)
        l_s[:rows, :] = jnp.full((rows, D), NEG, F32)

        def one_slot(slot, carry):
            count = meta_ref[slot]
            for fewest, blocks in ((1, 2), (3, 4), (5, 6), (7, 8)):

                @pl.when((count >= fewest) & (count <= blocks))
                def _():
                    attend_slot(slot, count, rows, blocks, fewest)

            return carry

        lax.fori_loop(0, 2, one_slot, 0)
        within = lanes_of((rows, 128)) & 7
        stats = jnp.zeros((rows, 128), F32)
        for p in range(H // 2):
            lse = l_s[:rows, 128 * p : 128 * (p + 1)]
            turned = pltpu.roll(lse, DH, 1)
            stats = jnp.where(within == 2 * p, lse, jnp.where(within == 2 * p + 1, turned, stats))
        packed = pack_stats(stats)
        value = v_s[:rows, :].astype(BF)
        for k in range(regions):
            e = list_ref[1, k]
            out_s[e, :, :D] = value[HALF * k : HALF * (k + 1)]
            out_s[e, :, D:] = packed[HALF * k : HALF * (k + 1)]

    sizes = [r for r in (8, 12, 16, 24) if r <= limit]
    for below, regions in zip([0] + sizes, sizes):

        @pl.when((seen > below) & (seen <= regions))
        def _():
            run(regions)

    for j, out in enumerate(outs):
        out[...] = out_s[NZ * j : NZ * (j + 1)]


def attend(shifts, meta, seen_by, near, keys, values):
    scalars = pl.BlockSpec(memory_space=pltpu.SMEM)
    vectors = pl.BlockSpec(memory_space=pltpu.VMEM)
    limit = NZ * len(shifts)
    return pl.pallas_call(
        functools.partial(attend_kernel, shifts),
        out_shape=[jax.ShapeDtypeStruct((NZ, HALF, WIDE), BF)] * len(shifts),
        in_specs=[scalars] * 2 + [vectors] * 3,
        out_specs=[vectors] * len(shifts),
        scratch_shapes=[
            pltpu.SMEM((2, 32), jnp.int32),
            pltpu.VMEM((limit * HALF, D), BF),
            pltpu.VMEM((limit * HALF, D), F32),
            pltpu.VMEM((limit * HALF, D), F32),
            pltpu.VMEM((limit, HALF, WIDE), BF),
        ],
        compiler_params=pltpu.CompilerParams(vmem_limit_bytes=ROOM),
        cost_estimate=pl.CostEstimate(flops=4 << 30, bytes_accessed=12 << 20, transcendentals=4 << 20),
        name="attend",
    )(meta, seen_by, near, keys, values)


def spread_matrix():
    row = lax.broadcasted_iota(jnp.int32, (128, WIDE), 0)
    col = lax.broadcasted_iota(jnp.int32, (128, WIDE), 1)
    head = jnp.where(col < D, col // DH, jnp.where(col < D + 24, col & 7, -1))
    return jnp.where((row < 24) & ((row & 7) == head), 1.0, 0.0).astype(BF)


def join(pieces, spread):
    lses = [jnp.dot(p[:, D:], spread, preferred_element_type=F32) for p in pieces]
    highest = functools.reduce(jnp.maximum, lses)
    scales = [jnp.exp(l - highest) for l in lses]
    total = functools.reduce(jnp.add, scales)
    value = functools.reduce(
        jnp.add, [p[:, :D].astype(F32) * s[:, :D] for p, s in zip(pieces, scales)]
    )
    return value / total[:, :D], (highest + jnp.log(total))[:, D:]


def join_kernel(*refs):
    *ins, out = refs
    pieces = [r[...] for r in ins] if len(ins) > 1 else [ins[0][k] for k in range(ins[0].shape[0])]
    value, lse = join(pieces, spread_matrix())
    out[..., :D] = jnp.broadcast_to(value.astype(BF), (*out.shape[:-1], D))
    out[..., D:] = jnp.broadcast_to(pack_stats(lse), (*out.shape[:-1], 128))


def joined(pieces, shape):
    return pl.pallas_call(
        join_kernel,
        out_shape=jax.ShapeDtypeStruct(shape, BF),
        in_specs=[pl.BlockSpec(memory_space=pltpu.VMEM)] * len(pieces),
        out_specs=pl.BlockSpec(memory_space=pltpu.VMEM),
        compiler_params=pltpu.CompilerParams(vmem_limit_bytes=ROOM),
        name="join_pieces",
    )(*pieces)


def final_kernel(place_ref, pieces_ref, lat_ref, gain_ref, wo_ref, own_ref, other_ref, out_ref, sums):
    row, core = place_ref[0], place_ref[1]
    pieces = [pieces_ref[k] for k in range(pieces_ref.shape[0])]
    value, _ = join(pieces, spread_matrix())
    attended = value.astype(BF)
    lat = lat_ref[pl.ds(pl.multiple_of(core * HALF, HALF), HALF), :]
    residual = lat.astype(F32) + jnp.dot(attended, wo_ref[...], preferred_element_type=F32)
    normed = norm_rows(residual, gain_ref[...]).astype(BF)
    for side, ref in enumerate((own_ref, other_ref)):
        for k in range(4):
            v = jnp.dot(normed, ref[k, :, :256], preferred_element_type=F32)
            hidden = jax.nn.gelu(v, approximate=True).astype(BF)
            down = jnp.concatenate([ref[k, :256, 256:], ref[k, 256:, 256:]], 1)
            at = 4 * side + lax.rem(row - k + 4, 4)
            sums[at] = jnp.dot(hidden, down, preferred_element_type=F32)
    total = residual
    for k in range(8):
        total = total + sums[k]
    out_ref[...] = total.astype(BF)


def shifted_x(a, by):
    pairs = [
        (zz * NX + xx, zz * NX + (xx + by) % NX) for zz in range(NZ) for xx in range(NX)
    ]
    return lax.ppermute(a, "region", pairs) if by % NX else a


def shifted_y(a, by):
    return lax.ppermute(a, "tm", [(k, (k + 2 * by) % 8) for k in range(8)]) if by % 4 else a


def core_swapped(a):
    return lax.ppermute(a, "tm", [(k, k ^ 1) for k in range(8)])


def on_device(
    observations,
    counts,
    visible,
    latents,
    lat_gain,
    mlp_gain,
    w_query,
    w_keyval,
    w_out,
    w_up,
    w_down,
):
    own = lax.axis_index("region")
    slot = lax.axis_index("tm")
    x, row, core = own % NX, slot // 2, slot % 2
    observed = observations[0, 0]
    lat = latents[0]
    scalars = pl.BlockSpec(memory_space=pltpu.SMEM)
    vectors = pl.BlockSpec(memory_space=pltpu.VMEM)

    with jax.named_scope("queries"):
        q = pl.pallas_call(
            query_kernel,
            out_shape=jax.ShapeDtypeStruct((NZ * NX, HALF, D), BF),
            in_specs=[scalars] + [vectors] * 3,
            out_specs=vectors,
            scratch_shapes=[pltpu.VMEM((LR, D), BF)],
            name="queries",
        )(core[None], lat, lat_gain[None], w_query)
    with jax.named_scope("gather"):
        near = lax.all_to_all(q, "region", 0, 0, tiled=True)

    with jax.named_scope("keyval"):
        other = core_swapped(observed)
        count = counts[0, 0]
        other_count = core_swapped(count)
        length = observed.shape[0]
        block = pl.BlockSpec((BLK, D), lambda i: (i, 0))
        keys, values, mlp = pl.pallas_call(
            keyval_kernel,
            grid=(length // BLK,),
            out_shape=[
                jax.ShapeDtypeStruct((2, length, D), BF),
                jax.ShapeDtypeStruct((2, length, 2 * D), BF),
                jax.ShapeDtypeStruct((D, D), BF),
            ],
            in_specs=[
                block,
                block,
                pl.BlockSpec((D, 2 * D), lambda i: (0, 0)),
                pl.BlockSpec((D, 256), lambda i: (0, 0)),
                pl.BlockSpec((256, D), lambda i: (0, 0)),
            ],
            out_specs=[
                pl.BlockSpec((2, BLK, D), lambda i: (0, i, 0)),
                pl.BlockSpec((2, BLK, 2 * D), lambda i: (0, i, 0)),
                pl.BlockSpec((D, D), lambda i: (0, 0)),
            ],
            compiler_params=pltpu.CompilerParams(vmem_limit_bytes=ROOM),
            cost_estimate=pl.CostEstimate(flops=4 << 30, bytes_accessed=18 << 20, transcendentals=0),
            name="keyval",
        )(observed, other, w_keyval, w_up, w_down)

    with jax.named_scope("weights"):
        shards = [shifted_y(mlp, k) for k in range(4)]

    seen_by = lax.dynamic_slice_in_dim(visible, own, 1, 1)[:, 0]
    meta = jnp.stack([count, other_count, own, x]).astype(jnp.int32)
    with jax.named_scope("attend"):
        pieces = []
        for shifts in ((2, 1, 3), (0,)):
            parts = attend(shifts, meta, seen_by, near, keys, values)
            for d, part in zip(shifts, parts):
                pieces.append(shifted_x(part.reshape(NZ * HALF, WIDE), -d))
    with jax.named_scope("join_x"):
        part = joined(pieces, (NZ * HALF, WIDE))
        part, *shards = lax.optimization_barrier((part, *shards))
    with jax.named_scope("join_z"):
        groups = [[zz * NX + xx for zz in range(NZ)] for xx in range(NX)]
        part = lax.all_to_all(
            part.reshape(NZ, HALF, WIDE), "region", 0, 0, axis_index_groups=groups, tiled=True
        )
        part = joined([part], (4, HALF, WIDE))
    with jax.named_scope("weights"):
        near_shards = jnp.stack(shards)
        far_shards = core_swapped(near_shards)
    with jax.named_scope("join_t"):
        groups = [[2 * k + c for k in range(4)] for c in range(2)]
        pieces = lax.all_to_all(part, "tm", 0, 0, axis_index_groups=groups, tiled=True)
    with jax.named_scope("final"):
        mine = pl.pallas_call(
            final_kernel,
            out_shape=jax.ShapeDtypeStruct((HALF, D), BF),
            in_specs=[scalars] + [vectors] * 6,
            out_specs=vectors,
            scratch_shapes=[pltpu.VMEM((8, HALF, D), F32)],
            compiler_params=pltpu.CompilerParams(vmem_limit_bytes=ROOM),
            name="final",
        )(jnp.stack([row, core]), pieces, lat, mlp_gain[None], w_out, near_shards, far_shards)
        theirs = core_swapped(mine)
        first = jnp.where(core == 0, mine, theirs)
        second = jnp.where(core == 0, theirs, mine)
    return jnp.concatenate([first, second])[None]


def solution(mesh):
    placed = (
        P("region", "tm", None, None),
        P("region", "tm"),
        P(),
        P("region", None, None),
        P(),
        P(),
        P(),
        P(),
        P(),
        P(None, "tm"),
        P("tm", None),
    )
    return jax.shard_map(
        on_device, mesh=mesh, in_specs=placed, out_specs=P("region", None, None), check_vma=False
    )
```

```python
import functools

import jax
import jax.numpy as jnp
from jax import lax
from jax.experimental import pallas as pl
from jax.experimental.pallas import tpu as pltpu
from jax.sharding import PartitionSpec as P

H = 8
BLK = 256
NZ, NX = 8, 4
EPS = 1e-05
NEG = -1e30
D = 512
DH = 64
LR = 32
WIDE = D + 128
HALF = LR // 2
ROOM = 28 << 20
BF = jnp.bfloat16
F32 = jnp.float32


def lanes_of(shape):
    return lax.broadcasted_iota(jnp.int32, shape, len(shape) - 1)


def norm_rows(values, gain):
    average = jnp.mean(values, axis=-1, keepdims=True)
    centered = values - average
    variance = jnp.mean(centered * centered, axis=-1, keepdims=True)
    return centered * lax.rsqrt(variance + EPS) * gain


def whole(shape):
    return pl.BlockSpec(shape, lambda *_: (0,) * len(shape))


def query_kernel(half_ref, lat_ref, gain_ref, wq_ref, out_ref, q_s):
    normed = norm_rows(lat_ref[...].astype(F32), gain_ref[...]).astype(BF)
    q = jnp.dot(normed, wq_ref[...], preferred_element_type=F32).astype(BF)
    q_s[...] = q * jnp.asarray(DH ** -0.5, BF)
    rows = q_s[pl.ds(pl.multiple_of(half_ref[0] * 16, 16), 16), :]
    out_ref[...] = jnp.broadcast_to(rows[None], out_ref.shape)


def keyval_kernel(mine_ref, other_ref, w_ref, up_ref, down_ref, kv_ref, mlp_ref):
    @pl.when(pl.program_id(0) == 0)
    def _():
        mlp_ref[:, :256] = up_ref[...]
        mlp_ref[:256, 256:] = down_ref[:, :256]
        mlp_ref[256:, 256:] = down_ref[:, 256:]

    for slot, obs_ref in enumerate((mine_ref, other_ref)):
        kv_ref[slot] = jnp.dot(obs_ref[...], w_ref[...], preferred_element_type=F32).astype(BF)


def pack_stats(lse):
    lane = lanes_of(lse.shape)
    high = lse.astype(BF).astype(F32)
    rest = lse - high
    mid = rest.astype(BF).astype(F32)
    low = rest - mid
    kept = jnp.where(lane < 8, high, jnp.where(lane < 16, mid, jnp.where(lane < 24, low, 0.0)))
    return kept.astype(BF)


def attend_kernel(shifts, meta_ref, vis_ref, near_ref, kv_in, *rest):
    outs, rest = rest[: len(shifts)], rest[len(shifts) :]
    kv_ref, list_ref, q_s, v_s, st_s, out_s, sems = rest
    copies = []
    for p in range(H // 2):
        parts = [pl.ds(128 * p, 128), pl.ds(D + 128 * p, 128)]
        copies.append(
            [
                pltpu.make_async_copy(kv_in.at[:, :, part], kv_ref.at[:, :, part], sems.at[k, p])
                for k, part in enumerate(parts)
            ]
        )
        for copy in copies[-1]:
            copy.start()
    counts = meta_ref[0], meta_ref[1]
    most = jnp.maximum(counts[0], counts[1])
    own, x = meta_ref[2], meta_ref[3]
    limit = NZ * len(shifts)
    columns = [lax.rem(x - d + NX, NX) for d in shifts]
    seen = jnp.int32(0)
    for j, column in enumerate(columns):
        for e in range(NZ):
            region = e * NX + column
            list_ref[0, seen] = region
            list_ref[1, seen] = jnp.int32(j * NZ + e)
            sees = (vis_ref[region] > 0) | (region == own)
            seen = seen + sees.astype(jnp.int32)
    last = jnp.maximum(seen - 1, 0)
    for k in range(limit):
        q_s[HALF * k : HALF * (k + 1), :] = near_ref[list_ref[0, jnp.minimum(k, last)]]

    lane = lanes_of((HALF, 128))
    out_s[:, :, :D] = jnp.zeros((limit, HALF, D), BF)
    out_s[:, :, D:] = jnp.broadcast_to(
        jnp.where(lane < 8, NEG, 0.0).astype(BF)[None], (limit, HALF, 128)
    )

    def pair(p, rows, blocks):
        keys = blocks * BLK
        low_half = lanes_of((rows, 128)) < DH
        here = pl.ds(pl.multiple_of(128 * p, 128), 128)
        there = pl.ds(pl.multiple_of(D + 128 * p, 128), 128)
        qp = q_s[:rows, here]
        zero = jnp.zeros_like(qp)
        both = jnp.concatenate([jnp.where(low_half, qp, zero), jnp.where(low_half, zero, qp)], 0)
        slots = []
        for slot in range(2):
            scores = lax.dot_general(
                both, kv_ref[slot, :keys, here], (((1,), (1,)), ((), ())), preferred_element_type=F32
            )
            parts = [scores[:, :BLK]]
            for j in range(1, blocks):
                parts.append(jnp.where(counts[slot] > j, scores[:, j * BLK : (j + 1) * BLK], NEG))
            slots.append(jnp.concatenate(parts, 1))
        peak = jnp.maximum(*[jnp.max(scores, axis=-1, keepdims=True) for scores in slots])
        even = odd = total = None
        for slot, scores in enumerate(slots):
            weights = jnp.exp(scores - peak)
            added = jnp.sum(weights, axis=-1, keepdims=True)
            weights, v = weights.astype(BF), kv_ref[slot, :keys, there]
            e = jnp.dot(weights[:rows], v, preferred_element_type=F32)
            o = jnp.dot(weights[rows:], v, preferred_element_type=F32)
            total = added if total is None else total + added
            even = e if even is None else even + e
            odd = o if odd is None else odd + o
        value = jnp.where(low_half, even / total[:rows], odd / total[rows:])
        v_s[:rows, here] = value.astype(BF)
        lse = peak + jnp.log(total)
        within = lanes_of((rows, 128)) & 7
        st_s[:rows, :] = jnp.where(
            within == 2 * p, lse[:rows], jnp.where(within == 2 * p + 1, lse[rows:], st_s[:rows, :])
        )

    sizes = [r for r in (12, 16, 24) if r <= limit] or [limit]

    def one_pair(p, carry):
        for q in range(H // 2):

            @pl.when(p == q)
            def _():
                for copy in copies[q]:
                    copy.wait()

        for blocks in (2, 8):
            for below, regions in zip([0] + sizes, sizes):
                fits = (seen > below) & (seen <= regions)

                @pl.when(fits & ((most <= 2) if blocks == 2 else (most > 2)))
                def _():
                    pair(p, regions * HALF, blocks)

        return carry

    lax.fori_loop(0, H // 2, one_pair, 0)
    for k in range(limit):

        @pl.when(k < seen)
        def _():
            e = list_ref[1, k]
            out_s[e, :, :D] = v_s[HALF * k : HALF * (k + 1), :]
            out_s[e, :, D:] = pack_stats(st_s[HALF * k : HALF * (k + 1), :])

    for j, out in enumerate(outs):
        out[...] = out_s[NZ * j : NZ * (j + 1)]


def attend(shifts, meta, seen_by, near, keyval):
    scalars = pl.BlockSpec(memory_space=pltpu.SMEM)
    vectors = pl.BlockSpec(memory_space=pltpu.VMEM)
    source = pl.BlockSpec(memory_space=pltpu.HBM)
    limit = NZ * len(shifts)
    return pl.pallas_call(
        functools.partial(attend_kernel, shifts),
        out_shape=[jax.ShapeDtypeStruct((NZ, HALF, WIDE), BF)] * len(shifts),
        in_specs=[scalars] * 2 + [vectors, source],
        out_specs=[vectors] * len(shifts),
        scratch_shapes=[
            pltpu.VMEM(keyval.shape, BF),
            pltpu.SMEM((2, 32), jnp.int32),
            pltpu.VMEM((limit * HALF, D), BF),
            pltpu.VMEM((limit * HALF, D), BF),
            pltpu.VMEM((limit * HALF, 128), F32),
            pltpu.VMEM((limit, HALF, WIDE), BF),
            pltpu.SemaphoreType.DMA((2, H // 2)),
        ],
        compiler_params=pltpu.CompilerParams(vmem_limit_bytes=58 << 20),
        cost_estimate=pl.CostEstimate(flops=4 << 30, bytes_accessed=12 << 20, transcendentals=4 << 20),
        name="attend",
    )(meta, seen_by, near, keyval)


def spread_matrix():
    row = lax.broadcasted_iota(jnp.int32, (128, WIDE), 0)
    col = lax.broadcasted_iota(jnp.int32, (128, WIDE), 1)
    head = jnp.where(col < D, col // DH, jnp.where(col < D + 24, col & 7, -1))
    return jnp.where((row < 24) & ((row & 7) == head), 1.0, 0.0).astype(BF)


def join(pieces, spread):
    lses = [jnp.dot(p[:, D:], spread, preferred_element_type=F32) for p in pieces]
    highest = functools.reduce(jnp.maximum, lses)
    scales = [jnp.exp(l - highest) for l in lses]
    total = functools.reduce(jnp.add, scales)
    value = functools.reduce(
        jnp.add, [p[:, :D].astype(F32) * s[:, :D] for p, s in zip(pieces, scales)]
    )
    return value / total[:, :D], (highest + jnp.log(total))[:, D:]


def join_kernel(*refs):
    *ins, out = refs
    pieces = [r[...] for r in ins] if len(ins) > 1 else [ins[0][k] for k in range(ins[0].shape[0])]
    value, lse = join(pieces, spread_matrix())
    out[..., :D] = jnp.broadcast_to(value.astype(BF), (*out.shape[:-1], D))
    out[..., D:] = jnp.broadcast_to(pack_stats(lse), (*out.shape[:-1], 128))


def joined(pieces, shape):
    return pl.pallas_call(
        join_kernel,
        out_shape=jax.ShapeDtypeStruct(shape, BF),
        in_specs=[pl.BlockSpec(memory_space=pltpu.VMEM)] * len(pieces),
        out_specs=pl.BlockSpec(memory_space=pltpu.VMEM),
        compiler_params=pltpu.CompilerParams(vmem_limit_bytes=ROOM),
        name="join_pieces",
    )(*pieces)


def final_kernel(row_ref, pieces_ref, lat_ref, gain_ref, wo_ref, *refs):
    weights, (res_ref, part_ref, sums) = refs[:4], refs[4:]
    spread = spread_matrix()
    halves = [join([pieces_ref[2 * k + c] for k in range(4)], spread)[0] for c in range(2)]
    attended = jnp.concatenate(halves, 0).astype(BF)
    residual = lat_ref[...].astype(F32) + jnp.dot(attended, wo_ref[...], preferred_element_type=F32)
    normed = norm_rows(residual, gain_ref[...]).astype(BF)
    res_ref[...] = residual
    for k, w in enumerate(weights):
        v = jnp.dot(normed, w[:, :256], preferred_element_type=F32)
        hidden = jax.nn.gelu(v, approximate=True).astype(BF)
        down = jnp.concatenate([w[:256, 256:], w[256:, 256:]], 1)
        sums[lax.rem(row_ref[0] - k + 4, 4)] = jnp.dot(hidden, down, preferred_element_type=F32)
    part_ref[...] = (sums[0] + sums[1]) + (sums[2] + sums[3])


def shifted_x(a, by):
    pairs = [
        (zz * NX + xx, zz * NX + (xx + by) % NX) for zz in range(NZ) for xx in range(NX)
    ]
    return lax.ppermute(a, "region", pairs) if by % NX else a


def shifted_y(a, by):
    return lax.ppermute(a, "tm", [(k, (k + 2 * by) % 8) for k in range(8)]) if by % 4 else a


def core_swapped(a):
    return lax.ppermute(a, "tm", [(k, k ^ 1) for k in range(8)])


def on_device(
    observations,
    counts,
    visible,
    latents,
    lat_gain,
    mlp_gain,
    w_query,
    w_keyval,
    w_out,
    w_up,
    w_down,
):
    own = lax.axis_index("region")
    slot = lax.axis_index("tm")
    x, row, core = own % NX, slot // 2, slot % 2
    observed = observations[0, 0]
    lat = latents[0]
    scalars = pl.BlockSpec(memory_space=pltpu.SMEM)
    vectors = pl.BlockSpec(memory_space=pltpu.VMEM)

    with jax.named_scope("queries"):
        q = pl.pallas_call(
            query_kernel,
            out_shape=jax.ShapeDtypeStruct((NZ * NX, HALF, D), BF),
            in_specs=[scalars] + [vectors] * 3,
            out_specs=vectors,
            scratch_shapes=[pltpu.VMEM((LR, D), BF)],
            name="queries",
        )(core[None], lat, lat_gain[None], w_query)
    with jax.named_scope("gather"):
        near = lax.all_to_all(q, "region", 0, 0, tiled=True)

    with jax.named_scope("keyval"):
        other = core_swapped(observed)
        count = counts[0, 0]
        other_count = core_swapped(count)
        length = observed.shape[0]
        block = pl.BlockSpec((BLK, D), lambda i: (i, 0))
        keyval, mlp = pl.pallas_call(
            keyval_kernel,
            grid=(length // BLK,),
            out_shape=[
                jax.ShapeDtypeStruct((2, length, 2 * D), BF),
                jax.ShapeDtypeStruct((D, D), BF),
            ],
            in_specs=[
                block,
                block,
                pl.BlockSpec((D, 2 * D), lambda i: (0, 0)),
                pl.BlockSpec((D, 256), lambda i: (0, 0)),
                pl.BlockSpec((256, D), lambda i: (0, 0)),
            ],
            out_specs=[
                pl.BlockSpec((2, BLK, 2 * D), lambda i: (0, i, 0)),
                pl.BlockSpec((D, D), lambda i: (0, 0)),
            ],
            compiler_params=pltpu.CompilerParams(vmem_limit_bytes=58 << 20),
            cost_estimate=pl.CostEstimate(flops=4 << 30, bytes_accessed=18 << 20, transcendentals=0),
            name="keyval",
        )(observed, other, w_keyval, w_up, w_down)

    with jax.named_scope("weights"):
        shards = [shifted_y(mlp, k) for k in range(4)]

    seen_by = lax.dynamic_slice_in_dim(visible, own, 1, 1)[:, 0]
    meta = jnp.stack([count, other_count, own, x]).astype(jnp.int32)
    with jax.named_scope("attend"):
        far_columns, near_columns = (2, 1, 3), (0,)
        parts = attend(far_columns, meta, seen_by, near, keyval)
        pieces = [
            shifted_x(part.reshape(NZ * HALF, WIDE), -d) for d, part in zip(far_columns, parts)
        ]
        meta, *shards = lax.optimization_barrier((meta, *shards))
        (part,) = attend(near_columns, meta, seen_by, near, keyval)
        pieces.append(part.reshape(NZ * HALF, WIDE))
    with jax.named_scope("join_x"):
        part = joined(pieces, (NZ * HALF, WIDE))
    with jax.named_scope("join_z"):
        groups = [[zz * NX + xx for zz in range(NZ)] for xx in range(NX)]
        part = lax.all_to_all(
            part.reshape(NZ, HALF, WIDE), "region", 0, 0, axis_index_groups=groups, tiled=True
        )
        part = joined([part], (8, HALF, WIDE))
    with jax.named_scope("join_t"):
        pieces = lax.all_to_all(part, "tm", 0, 0, tiled=True)
    with jax.named_scope("final"):
        residual, mine = pl.pallas_call(
            final_kernel,
            out_shape=[jax.ShapeDtypeStruct((LR, D), F32)] * 2,
            in_specs=[scalars] + [vectors] * 8,
            out_specs=[vectors] * 2,
            scratch_shapes=[pltpu.VMEM((4, LR, D), F32)],
            compiler_params=pltpu.CompilerParams(vmem_limit_bytes=ROOM),
            name="final",
        )(row[None], pieces, lat, mlp_gain[None], w_out, *shards)
        out = residual + (mine + core_swapped(mine))
    return out.astype(BF)[None]


def solution(mesh):
    placed = (
        P("region", "tm", None, None),
        P("region", "tm"),
        P(),
        P("region", None, None),
        P(),
        P(),
        P(),
        P(),
        P(),
        P(None, "tm"),
        P("tm", None),
    )
    return jax.shard_map(
        on_device, mesh=mesh, in_specs=placed, out_specs=P("region", None, None), check_vma=False
    )
```

```python
import functools

import jax
import jax.numpy as jnp
from jax import lax
from jax.experimental import pallas as pl
from jax.experimental.pallas import tpu as pltpu
from jax.sharding import PartitionSpec as P

H = 8
BLK = 256
NZ, NX = 8, 4
EPS = 1e-05
NEG = -1e30
D = 512
DH = 64
LR = 32
WIDE = D + 128
BF = jnp.bfloat16
F32 = jnp.float32


def lanes_of(shape):
    return lax.broadcasted_iota(jnp.int32, shape, len(shape) - 1)


def norm_rows(values, gain):
    average = jnp.mean(values, axis=-1, keepdims=True)
    centered = values - average
    variance = jnp.mean(centered * centered, axis=-1, keepdims=True)
    return centered * lax.rsqrt(variance + EPS) * gain


def whole(shape):
    return pl.BlockSpec(shape, lambda *_: (0,) * len(shape))


def query_kernel(half_ref, lat_ref, gain_ref, wq_ref, out_ref, q_s):
    normed = norm_rows(lat_ref[...].astype(F32), gain_ref[...]).astype(BF)
    q = jnp.dot(normed, wq_ref[...], preferred_element_type=F32).astype(BF)
    q_s[...] = q * jnp.asarray(DH ** -0.5, BF)
    rows = q_s[pl.ds(pl.multiple_of(half_ref[0] * 16, 16), 16), :]
    out_ref[...] = jnp.broadcast_to(rows[None], out_ref.shape)


def keyval_kernel(obs_ref, w_ref, up_ref, down_ref, k_ref, va_ref, mlp_ref):
    @pl.when(pl.program_id(0) == 0)
    def _():
        mlp_ref[:, :256] = up_ref[...]
        mlp_ref[:256, 256:] = down_ref[:, :256]
        mlp_ref[256:, 256:] = down_ref[:, 256:]

    kv = jnp.dot(obs_ref[...], w_ref[...], preferred_element_type=F32).astype(BF)
    k_ref[...] = kv[:, :D]
    low_half = lanes_of((kv.shape[0], 128)) < DH
    ones = jnp.ones((kv.shape[0], 128), BF)
    for p in range(H // 2):
        v = kv[:, D + 128 * p : D + 128 * (p + 1)]
        va_ref[:, 256 * p : 256 * p + 128] = jnp.where(low_half, v, ones)
        va_ref[:, 256 * p + 128 : 256 * p + 256] = jnp.where(low_half, ones, v)


def pack_stats(lse):
    lane = lanes_of(lse.shape)
    high = lse.astype(BF).astype(F32)
    rest = lse - high
    mid = rest.astype(BF).astype(F32)
    low = rest - mid
    kept = jnp.where(lane < 8, high, jnp.where(lane < 16, mid, jnp.where(lane < 24, low, 0.0)))
    return kept.astype(BF)


def attend_kernel(shift, meta_ref, vis_ref, near_ref, far_ref, k_ref, va_ref, out_ref, list_ref, q_s):
    count = meta_ref[0]
    own, core = meta_ref[1], meta_ref[2]
    column = lax.rem(meta_ref[3] - shift + NX, NX)
    seen = jnp.int32(0)
    for e in range(NZ):
        region = e * NX + column
        list_ref[seen] = jnp.int32(e)
        sees = (vis_ref[region] > 0) | (region == own)
        seen = seen + sees.astype(jnp.int32)
    last = list_ref[jnp.maximum(seen - 1, 0)]
    for k in range(3):
        list_ref[seen + k] = last

    lane = lanes_of((LR, 128))
    out_ref[:, :, :D] = jnp.zeros((NZ, LR, D), BF)
    out_ref[:, :, D:] = jnp.broadcast_to(
        jnp.where(lane < 8, NEG, 0.0).astype(BF)[None], (NZ, LR, 128)
    )

    def group(start, regions, blocks, unroll):
        keys, rows = blocks * BLK, regions * LR
        entries = [list_ref[start + k] for k in range(regions)]
        for k, e in enumerate(entries):
            region = e * NX + column
            q_s[pl.ds(pl.multiple_of(32 * k + 16 * core, 16), 16), :] = near_ref[region]
            q_s[pl.ds(pl.multiple_of(32 * k + 16 - 16 * core, 16), 16), :] = far_ref[region]
        wide = lanes_of((rows, 128))
        low_half = wide < DH
        sure = max(1, blocks // 2 + (blocks > 2))

        def pair(p, stats):
            here = pl.ds(pl.multiple_of(128 * p, 128), 128)
            even_at = pl.ds(pl.multiple_of(256 * p, 128), 128)
            odd_at = pl.ds(pl.multiple_of(256 * p + 128, 128), 128)
            qp = q_s[:rows, here]
            zero = jnp.zeros_like(qp)
            both = jnp.concatenate([jnp.where(low_half, qp, zero), jnp.where(low_half, zero, qp)], 0)
            scores = lax.dot_general(
                both, k_ref[:keys, here], (((1,), (1,)), ((), ())), preferred_element_type=F32
            )
            parts = [scores[:, : sure * BLK]]
            for j in range(sure, blocks):
                parts.append(jnp.where(count > j, scores[:, j * BLK : (j + 1) * BLK], NEG))
            scores = jnp.concatenate(parts, 1)
            peak = jnp.max(scores, axis=-1, keepdims=True)
            weights = jnp.exp(scores - peak).astype(BF)
            even = jnp.dot(weights[:rows], va_ref[:keys, even_at], preferred_element_type=F32)
            odd = jnp.dot(weights[rows:], va_ref[:keys, odd_at], preferred_element_type=F32)
            total = pltpu.roll(jnp.where(low_half, odd, even), DH, 1)
            value = (jnp.where(low_half, even, odd) / total).astype(BF)
            lse = jnp.where(low_half, peak[:rows], peak[rows:]) + jnp.log(total)
            turned = pltpu.roll(lse, DH, 1)
            within = wide & 7
            stats = jnp.where(within == 2 * p, lse, jnp.where(within == 2 * p + 1, turned, stats))
            for k, e in enumerate(entries):
                out_ref[e, :, here] = value[32 * k : 32 * (k + 1)]
            return stats

        def pairs(i, stats):
            for k in range(unroll):
                stats = pair(i * unroll + k, stats)
            return stats

        stats = lax.fori_loop(0, H // 2 // unroll, pairs, jnp.zeros((rows, 128), F32))
        packed = pack_stats(stats)
        for k, e in enumerate(entries):
            out_ref[e, :, D:] = packed[32 * k : 32 * (k + 1)]

    for least, blocks in ((1, 2), (3, 4)):

        @pl.when((count >= least) & (count <= blocks))
        def _():
            def body(g, carry):
                group(4 * g, 4, blocks, 1)
                return carry

            lax.fori_loop(0, (seen + 3) // 4, body, 0)

    for fewest, regions, unroll in ((1, 4, 1), (5, 6, 2), (7, 8, 1)):

        @pl.when((count > 4) & (seen >= fewest) & (seen <= regions))
        def _():
            group(0, regions, 8, unroll)


def attend(shift, meta, seen_by, near, far, keys, values):
    scalars = pl.BlockSpec(memory_space=pltpu.SMEM)
    vectors = pl.BlockSpec(memory_space=pltpu.VMEM)
    return pl.pallas_call(
        functools.partial(attend_kernel, shift),
        out_shape=jax.ShapeDtypeStruct((NZ, LR, WIDE), BF),
        in_specs=[scalars] * 2 + [vectors] * 4,
        out_specs=vectors,
        scratch_shapes=[pltpu.SMEM((16,), jnp.int32), pltpu.VMEM((256, D), BF)],
        compiler_params=pltpu.CompilerParams(vmem_limit_bytes=24 << 20),
        cost_estimate=pl.CostEstimate(flops=2 << 30, bytes_accessed=8 << 20, transcendentals=2 << 20),
        name="attend",
    )(meta, seen_by, near, far, keys, values)


def spread_matrix():
    row = lax.broadcasted_iota(jnp.int32, (128, WIDE), 0)
    col = lax.broadcasted_iota(jnp.int32, (128, WIDE), 1)
    head = jnp.where(col < D, col // DH, jnp.where(col < D + 24, col & 7, -1))
    return jnp.where((row < 24) & ((row & 7) == head), 1.0, 0.0).astype(BF)


def join(pieces, spread):
    lses = [jnp.dot(p[:, D:], spread, preferred_element_type=F32) for p in pieces]
    highest = functools.reduce(jnp.maximum, lses)
    scales = [jnp.exp(l - highest) for l in lses]
    total = functools.reduce(jnp.add, scales)
    value = functools.reduce(
        jnp.add, [p[:, :D].astype(F32) * s[:, :D] for p, s in zip(pieces, scales)]
    )
    return value / total[:, :D], (highest + jnp.log(total))[:, D:]


def join_kernel(*refs):
    *ins, out = refs
    pieces = [r[...] for r in ins] if len(ins) > 1 else [ins[0][k] for k in range(ins[0].shape[0])]
    value, lse = join(pieces, spread_matrix())
    out[..., :D] = jnp.broadcast_to(value.astype(BF), (*out.shape[:-1], D))
    out[..., D:] = jnp.broadcast_to(pack_stats(lse), (*out.shape[:-1], 128))


def joined(pieces, shape):
    return pl.pallas_call(
        join_kernel,
        out_shape=jax.ShapeDtypeStruct(shape, BF),
        in_specs=[pl.BlockSpec(memory_space=pltpu.VMEM)] * len(pieces),
        out_specs=pl.BlockSpec(memory_space=pltpu.VMEM),
        compiler_params=pltpu.CompilerParams(vmem_limit_bytes=16 << 20),
        name="join_pieces",
    )(*pieces)


def final_kernel(row_ref, pieces_ref, lat_ref, gain_ref, wo_ref, *refs):
    weights, (res_ref, part_ref, sums) = refs[:4], refs[4:]
    pieces = [pieces_ref[k] for k in range(8)]
    value, _ = join(pieces, spread_matrix())
    attended = value.astype(BF)
    residual = lat_ref[...].astype(F32) + jnp.dot(attended, wo_ref[...], preferred_element_type=F32)
    normed = norm_rows(residual, gain_ref[...]).astype(BF)
    res_ref[...] = residual
    for k, w in enumerate(weights):
        v = jnp.dot(normed, w[:, :256], preferred_element_type=F32)
        hidden = jax.nn.gelu(v, approximate=True).astype(BF)
        down = jnp.concatenate([w[:256, 256:], w[256:, 256:]], 1)
        sums[lax.rem(row_ref[0] - k + 4, 4)] = jnp.dot(hidden, down, preferred_element_type=F32)
    part_ref[...] = (sums[0] + sums[1]) + (sums[2] + sums[3])


def shifted_x(a, by):
    pairs = [
        (zz * NX + xx, zz * NX + (xx + by) % NX) for zz in range(NZ) for xx in range(NX)
    ]
    return lax.ppermute(a, "region", pairs) if by % NX else a


def shifted_y(a, by):
    return lax.ppermute(a, "tm", [(k, (k + 2 * by) % 8) for k in range(8)]) if by % 4 else a


def core_swapped(a):
    return lax.ppermute(a, "tm", [(k, k ^ 1) for k in range(8)])


def on_device(
    observations,
    counts,
    visible,
    latents,
    lat_gain,
    mlp_gain,
    w_query,
    w_keyval,
    w_out,
    w_up,
    w_down,
):
    own = lax.axis_index("region")
    slot = lax.axis_index("tm")
    x, row, core = own % NX, slot // 2, slot % 2
    observed = observations[0, 0]
    lat = latents[0]
    scalars = pl.BlockSpec(memory_space=pltpu.SMEM)
    vectors = pl.BlockSpec(memory_space=pltpu.VMEM)

    with jax.named_scope("queries"):
        q = pl.pallas_call(
            query_kernel,
            out_shape=jax.ShapeDtypeStruct((NZ * NX, 16, D), BF),
            in_specs=[scalars] + [vectors] * 3,
            out_specs=vectors,
            scratch_shapes=[pltpu.VMEM((LR, D), BF)],
            name="queries",
        )(core[None], lat, lat_gain[None], w_query)
    with jax.named_scope("gather"):
        near = lax.all_to_all(q, "region", 0, 0, tiled=True)

    with jax.named_scope("keyval"):
        keys, values, mlp = pl.pallas_call(
            keyval_kernel,
            grid=(observed.shape[0] // BLK,),
            out_shape=[
                jax.ShapeDtypeStruct((observed.shape[0], D), BF),
                jax.ShapeDtypeStruct((observed.shape[0], 2 * D), BF),
                jax.ShapeDtypeStruct((D, D), BF),
            ],
            in_specs=[
                pl.BlockSpec((BLK, D), lambda i: (i, 0)),
                pl.BlockSpec((D, 2 * D), lambda i: (0, 0)),
                pl.BlockSpec((D, 256), lambda i: (0, 0)),
                pl.BlockSpec((256, D), lambda i: (0, 0)),
            ],
            out_specs=[
                pl.BlockSpec((BLK, D), lambda i: (i, 0)),
                pl.BlockSpec((BLK, 2 * D), lambda i: (i, 0)),
                pl.BlockSpec((D, D), lambda i: (0, 0)),
            ],
            compiler_params=pltpu.CompilerParams(vmem_limit_bytes=58 << 20),
            cost_estimate=pl.CostEstimate(flops=2 << 30, bytes_accessed=9 << 20, transcendentals=0),
            name="keyval",
        )(observed, w_keyval, w_up, w_down)

    seen_by = lax.dynamic_slice_in_dim(visible, own, 1, 1)[:, 0]
    meta = jnp.stack([counts[0, 0], own, core, x]).astype(jnp.int32)
    near, values, seen_by, meta = lax.optimization_barrier((near, values, seen_by, meta))
    with jax.named_scope("gather"):
        far = core_swapped(near)
    with jax.named_scope("weights"):
        shards = [shifted_y(mlp, k) for k in range(4)]

    with jax.named_scope("attend"):
        pieces = []
        for d in (2, 1, 3, 0):
            if d == 0:
                meta, *shards = lax.optimization_barrier((meta, *shards))
            part = attend(d, meta, seen_by, near, far, keys, values)
            pieces.append(shifted_x(part.reshape(NZ * LR, WIDE), -d))
    with jax.named_scope("join_x"):
        part = joined(pieces, (NZ * LR, WIDE)).reshape(NZ, LR, WIDE)
    with jax.named_scope("join_z"):
        groups = [[zz * NX + xx for zz in range(NZ)] for xx in range(NX)]
        part = lax.all_to_all(part, "region", 0, 0, axis_index_groups=groups, tiled=True)
        part = joined([part], (8, LR, WIDE))
    with jax.named_scope("join_t"):
        pieces = lax.all_to_all(part, "tm", 0, 0, tiled=True)
    with jax.named_scope("final"):
        residual, mine = pl.pallas_call(
            final_kernel,
            out_shape=[jax.ShapeDtypeStruct((LR, D), F32)] * 2,
            in_specs=[scalars] + [vectors] * 8,
            out_specs=[vectors] * 2,
            scratch_shapes=[pltpu.VMEM((4, LR, D), F32)],
            compiler_params=pltpu.CompilerParams(vmem_limit_bytes=16 << 20),
            name="final",
        )(row[None], pieces, lat, mlp_gain[None], w_out, *shards)
        out = residual + (mine + core_swapped(mine))
    return out.astype(BF)[None]


def solution(mesh):
    placed = (
        P("region", "tm", None, None),
        P("region", "tm"),
        P(),
        P("region", None, None),
        P(),
        P(),
        P(),
        P(),
        P(),
        P(None, "tm"),
        P("tm", None),
    )
    return jax.shard_map(
        on_device, mesh=mesh, in_specs=placed, out_specs=P("region", None, None), check_vma=False
    )
```

```python
import functools

import jax
import jax.numpy as jnp
from jax import lax
from jax.experimental import pallas as pl
from jax.experimental.pallas import tpu as pltpu
from jax.sharding import PartitionSpec as P

H = 8
BLK = 256
NZ, NX = 8, 4
EPS = 1e-05
NEG = -1e30
D = 512
DH = 64
LR = 32
WIDE = D + 128
BF = jnp.bfloat16
F32 = jnp.float32


def lanes_of(shape):
    return lax.broadcasted_iota(jnp.int32, shape, len(shape) - 1)


def norm_rows(values, gain):
    average = jnp.mean(values, axis=-1, keepdims=True)
    centered = values - average
    variance = jnp.mean(centered * centered, axis=-1, keepdims=True)
    return centered * lax.rsqrt(variance + EPS) * gain


def whole(shape):
    return pl.BlockSpec(shape, lambda *_: (0,) * len(shape))


def query_kernel(half_ref, lat_ref, gain_ref, wq_ref, out_ref, q_s):
    normed = norm_rows(lat_ref[...].astype(F32), gain_ref[...]).astype(BF)
    q = jnp.dot(normed, wq_ref[...], preferred_element_type=F32).astype(BF)
    q_s[...] = q * jnp.asarray(DH ** -0.5, BF)
    rows = q_s[pl.ds(pl.multiple_of(half_ref[0] * 16, 16), 16), :]
    out_ref[...] = jnp.broadcast_to(rows[None], out_ref.shape)


def keyval_kernel(obs_ref, w_ref, up_ref, down_ref, k_ref, va_ref, mlp_ref):
    @pl.when(pl.program_id(0) == 0)
    def _():
        mlp_ref[:, :256] = up_ref[...]
        mlp_ref[:256, 256:] = down_ref[:, :256]
        mlp_ref[256:, 256:] = down_ref[:, 256:]

    kv = jnp.dot(obs_ref[...], w_ref[...], preferred_element_type=F32).astype(BF)
    k_ref[...] = kv[:, :D]
    low_half = lanes_of((kv.shape[0], 128)) < DH
    ones = jnp.ones((kv.shape[0], 128), BF)
    for p in range(H // 2):
        v = kv[:, D + 128 * p : D + 128 * (p + 1)]
        va_ref[:, 256 * p : 256 * p + 128] = jnp.where(low_half, v, ones)
        va_ref[:, 256 * p + 128 : 256 * p + 256] = jnp.where(low_half, ones, v)


def pack_stats(lse):
    lane = lanes_of(lse.shape)
    high = lse.astype(BF).astype(F32)
    rest = lse - high
    mid = rest.astype(BF).astype(F32)
    low = rest - mid
    kept = jnp.where(lane < 8, high, jnp.where(lane < 16, mid, jnp.where(lane < 24, low, 0.0)))
    return kept.astype(BF)


def attend_kernel(shift, meta_ref, vis_ref, near_ref, far_ref, k_ref, va_ref, out_ref, list_ref, q_s):
    count = meta_ref[0]
    own, core = meta_ref[1], meta_ref[2]
    column = lax.rem(meta_ref[3] - shift + NX, NX)
    seen = jnp.int32(0)
    for e in range(NZ):
        region = e * NX + column
        list_ref[seen] = jnp.int32(e)
        sees = (vis_ref[region] > 0) | (region == own)
        seen = seen + sees.astype(jnp.int32)
    last = list_ref[jnp.maximum(seen - 1, 0)]
    for k in range(3):
        list_ref[seen + k] = last

    lane = lanes_of((LR, 128))
    out_ref[:, :, :D] = jnp.zeros((NZ, LR, D), BF)
    out_ref[:, :, D:] = jnp.broadcast_to(
        jnp.where(lane < 8, NEG, 0.0).astype(BF)[None], (NZ, LR, 128)
    )

    def group(start, regions, blocks, unroll):
        keys, rows = blocks * BLK, regions * LR
        entries = [list_ref[start + k] for k in range(regions)]
        for k, e in enumerate(entries):
            region = e * NX + column
            q_s[pl.ds(pl.multiple_of(32 * k + 16 * core, 16), 16), :] = near_ref[region]
            q_s[pl.ds(pl.multiple_of(32 * k + 16 - 16 * core, 16), 16), :] = far_ref[region]
        wide = lanes_of((rows, 128))
        low_half = wide < DH
        sure = max(1, blocks // 2 + (blocks > 2))

        def pair(p, stats):
            here = pl.ds(pl.multiple_of(128 * p, 128), 128)
            even_at = pl.ds(pl.multiple_of(256 * p, 128), 128)
            odd_at = pl.ds(pl.multiple_of(256 * p + 128, 128), 128)
            qp = q_s[:rows, here]
            zero = jnp.zeros_like(qp)
            both = jnp.concatenate([jnp.where(low_half, qp, zero), jnp.where(low_half, zero, qp)], 0)
            scores = lax.dot_general(
                both, k_ref[:keys, here], (((1,), (1,)), ((), ())), preferred_element_type=F32
            )
            parts = [scores[:, : sure * BLK]]
            for j in range(sure, blocks):
                parts.append(jnp.where(count > j, scores[:, j * BLK : (j + 1) * BLK], NEG))
            scores = jnp.concatenate(parts, 1)
            peak = jnp.max(scores, axis=-1, keepdims=True)
            weights = jnp.exp(scores - peak).astype(BF)
            even = jnp.dot(weights[:rows], va_ref[:keys, even_at], preferred_element_type=F32)
            odd = jnp.dot(weights[rows:], va_ref[:keys, odd_at], preferred_element_type=F32)
            total = pltpu.roll(jnp.where(low_half, odd, even), DH, 1)
            value = (jnp.where(low_half, even, odd) / total).astype(BF)
            lse = jnp.where(low_half, peak[:rows], peak[rows:]) + jnp.log(total)
            turned = pltpu.roll(lse, DH, 1)
            within = wide & 7
            stats = jnp.where(within == 2 * p, lse, jnp.where(within == 2 * p + 1, turned, stats))
            for k, e in enumerate(entries):
                out_ref[e, :, here] = value[32 * k : 32 * (k + 1)]
            return stats

        def pairs(i, stats):
            for k in range(unroll):
                stats = pair(i * unroll + k, stats)
            return stats

        stats = lax.fori_loop(0, H // 2 // unroll, pairs, jnp.zeros((rows, 128), F32))
        packed = pack_stats(stats)
        for k, e in enumerate(entries):
            out_ref[e, :, D:] = packed[32 * k : 32 * (k + 1)]

    for least, blocks in ((1, 2), (3, 4)):

        @pl.when((count >= least) & (count <= blocks))
        def _():
            def body(g, carry):
                group(4 * g, 4, blocks, 1)
                return carry

            lax.fori_loop(0, (seen + 3) // 4, body, 0)

    for fewest, regions, unroll in ((1, 4, 1), (5, 6, 2), (7, 8, 1)):

        @pl.when((count > 4) & (seen >= fewest) & (seen <= regions))
        def _():
            group(0, regions, 8, unroll)


def attend(shift, meta, seen_by, near, far, keys, values):
    scalars = pl.BlockSpec(memory_space=pltpu.SMEM)
    vectors = pl.BlockSpec(memory_space=pltpu.VMEM)
    return pl.pallas_call(
        functools.partial(attend_kernel, shift),
        out_shape=jax.ShapeDtypeStruct((NZ, LR, WIDE), BF),
        in_specs=[scalars] * 2 + [vectors] * 4,
        out_specs=vectors,
        scratch_shapes=[pltpu.SMEM((16,), jnp.int32), pltpu.VMEM((256, D), BF)],
        compiler_params=pltpu.CompilerParams(vmem_limit_bytes=24 << 20),
        cost_estimate=pl.CostEstimate(flops=2 << 30, bytes_accessed=8 << 20, transcendentals=2 << 20),
        name="attend",
    )(meta, seen_by, near, far, keys, values)


def spread_matrix():
    row = lax.broadcasted_iota(jnp.int32, (128, WIDE), 0)
    col = lax.broadcasted_iota(jnp.int32, (128, WIDE), 1)
    head = jnp.where(col < D, col // DH, jnp.where(col < D + 24, col & 7, -1))
    return jnp.where((row < 24) & ((row & 7) == head), 1.0, 0.0).astype(BF)


def join(pieces, spread):
    lses = [jnp.dot(p[:, D:], spread, preferred_element_type=F32) for p in pieces]
    highest = functools.reduce(jnp.maximum, lses)
    scales = [jnp.exp(l - highest) for l in lses]
    total = functools.reduce(jnp.add, scales)
    value = functools.reduce(
        jnp.add, [p[:, :D].astype(F32) * s[:, :D] for p, s in zip(pieces, scales)]
    )
    return value / total[:, :D], (highest + jnp.log(total))[:, D:]


def join_kernel(*refs):
    *ins, out = refs
    pieces = [r[...] for r in ins] if len(ins) > 1 else [ins[0][k] for k in range(ins[0].shape[0])]
    value, lse = join(pieces, spread_matrix())
    out[..., :D] = jnp.broadcast_to(value.astype(BF), (*out.shape[:-1], D))
    out[..., D:] = jnp.broadcast_to(pack_stats(lse), (*out.shape[:-1], 128))


def joined(pieces, shape):
    return pl.pallas_call(
        join_kernel,
        out_shape=jax.ShapeDtypeStruct(shape, BF),
        in_specs=[pl.BlockSpec(memory_space=pltpu.VMEM)] * len(pieces),
        out_specs=pl.BlockSpec(memory_space=pltpu.VMEM),
        compiler_params=pltpu.CompilerParams(vmem_limit_bytes=16 << 20),
        name="join_pieces",
    )(*pieces)


def final_kernel(row_ref, pieces_ref, lat_ref, gain_ref, wo_ref, *refs):
    weights, (res_ref, part_ref, sums) = refs[:4], refs[4:]
    pieces = [pieces_ref[k] for k in range(8)]
    value, _ = join(pieces, spread_matrix())
    attended = value.astype(BF)
    residual = lat_ref[...].astype(F32) + jnp.dot(attended, wo_ref[...], preferred_element_type=F32)
    normed = norm_rows(residual, gain_ref[...]).astype(BF)
    res_ref[...] = residual
    for k, w in enumerate(weights):
        v = jnp.dot(normed, w[:, :256], preferred_element_type=F32)
        hidden = jax.nn.gelu(v, approximate=True).astype(BF)
        down = jnp.concatenate([w[:256, 256:], w[256:, 256:]], 1)
        sums[lax.rem(row_ref[0] - k + 4, 4)] = jnp.dot(hidden, down, preferred_element_type=F32)
    part_ref[...] = (sums[0] + sums[1]) + (sums[2] + sums[3])


def shifted_x(a, by):
    pairs = [
        (zz * NX + xx, zz * NX + (xx + by) % NX) for zz in range(NZ) for xx in range(NX)
    ]
    return lax.ppermute(a, "region", pairs) if by % NX else a


def shifted_y(a, by):
    return lax.ppermute(a, "tm", [(k, (k + 2 * by) % 8) for k in range(8)]) if by % 4 else a


def core_swapped(a):
    return lax.ppermute(a, "tm", [(k, k ^ 1) for k in range(8)])


def on_device(
    observations,
    counts,
    visible,
    latents,
    lat_gain,
    mlp_gain,
    w_query,
    w_keyval,
    w_out,
    w_up,
    w_down,
):
    own = lax.axis_index("region")
    slot = lax.axis_index("tm")
    x, row, core = own % NX, slot // 2, slot % 2
    observed = observations[0, 0]
    lat = latents[0]
    scalars = pl.BlockSpec(memory_space=pltpu.SMEM)
    vectors = pl.BlockSpec(memory_space=pltpu.VMEM)

    with jax.named_scope("queries"):
        q = pl.pallas_call(
            query_kernel,
            out_shape=jax.ShapeDtypeStruct((NZ * NX, 16, D), BF),
            in_specs=[scalars] + [vectors] * 3,
            out_specs=vectors,
            scratch_shapes=[pltpu.VMEM((LR, D), BF)],
            name="queries",
        )(core[None], lat, lat_gain[None], w_query)
    with jax.named_scope("gather"):
        near = lax.all_to_all(q, "region", 0, 0, tiled=True)

    with jax.named_scope("keyval"):
        keys, values, mlp = pl.pallas_call(
            keyval_kernel,
            grid=(observed.shape[0] // BLK,),
            out_shape=[
                jax.ShapeDtypeStruct((observed.shape[0], D), BF),
                jax.ShapeDtypeStruct((observed.shape[0], 2 * D), BF),
                jax.ShapeDtypeStruct((D, D), BF),
            ],
            in_specs=[
                pl.BlockSpec((BLK, D), lambda i: (i, 0)),
                pl.BlockSpec((D, 2 * D), lambda i: (0, 0)),
                pl.BlockSpec((D, 256), lambda i: (0, 0)),
                pl.BlockSpec((256, D), lambda i: (0, 0)),
            ],
            out_specs=[
                pl.BlockSpec((BLK, D), lambda i: (i, 0)),
                pl.BlockSpec((BLK, 2 * D), lambda i: (i, 0)),
                pl.BlockSpec((D, D), lambda i: (0, 0)),
            ],
            compiler_params=pltpu.CompilerParams(vmem_limit_bytes=58 << 20),
            cost_estimate=pl.CostEstimate(flops=2 << 30, bytes_accessed=9 << 20, transcendentals=0),
            name="keyval",
        )(observed, w_keyval, w_up, w_down)

    seen_by = lax.dynamic_slice_in_dim(visible, own, 1, 1)[:, 0]
    meta = jnp.stack([counts[0, 0], own, core, x]).astype(jnp.int32)
    near, values, seen_by, meta = lax.optimization_barrier((near, values, seen_by, meta))
    with jax.named_scope("gather"):
        far = core_swapped(near)
    with jax.named_scope("attend"):
        pieces = []
        for d in (2, 1, 3, 0):
            part = attend(d, meta, seen_by, near, far, keys, values)
            pieces.append(shifted_x(part.reshape(NZ * LR, WIDE), -d))
    with jax.named_scope("join_x"):
        part = joined(pieces, (NZ * LR, WIDE)).reshape(NZ, LR, WIDE)
    part, mlp = lax.optimization_barrier((part, mlp))
    with jax.named_scope("weights"):
        shards = [shifted_y(mlp, k) for k in range(4)]
    with jax.named_scope("join_z"):
        groups = [[zz * NX + xx for zz in range(NZ)] for xx in range(NX)]
        part = lax.all_to_all(part, "region", 0, 0, axis_index_groups=groups, tiled=True)
        part = joined([part], (8, LR, WIDE))
    with jax.named_scope("join_t"):
        pieces = lax.all_to_all(part, "tm", 0, 0, tiled=True)
    with jax.named_scope("final"):
        residual, mine = pl.pallas_call(
            final_kernel,
            out_shape=[jax.ShapeDtypeStruct((LR, D), F32)] * 2,
            in_specs=[scalars] + [vectors] * 8,
            out_specs=[vectors] * 2,
            scratch_shapes=[pltpu.VMEM((4, LR, D), F32)],
            compiler_params=pltpu.CompilerParams(vmem_limit_bytes=16 << 20),
            name="final",
        )(row[None], pieces, lat, mlp_gain[None], w_out, *shards)
        out = residual + (mine + core_swapped(mine))
    return out.astype(BF)[None]


def solution(mesh):
    placed = (
        P("region", "tm", None, None),
        P("region", "tm"),
        P(),
        P("region", None, None),
        P(),
        P(),
        P(),
        P(),
        P(),
        P(None, "tm"),
        P("tm", None),
    )
    return jax.shard_map(
        on_device, mesh=mesh, in_specs=placed, out_specs=P("region", None, None), check_vma=False
    )
```

```python
import functools

import jax
import jax.numpy as jnp
from jax import lax
from jax.experimental import pallas as pl
from jax.experimental.pallas import tpu as pltpu
from jax.sharding import PartitionSpec as P

H = 8
BLK = 256
NZ, NX = 8, 4
EPS = 1e-05
NEG = -1e30
D = 512
DH = 64
LR = 32
WIDE = D + 128
BF = jnp.bfloat16
F32 = jnp.float32


def lanes_of(shape):
    return lax.broadcasted_iota(jnp.int32, shape, len(shape) - 1)


def norm_rows(values, gain):
    average = jnp.mean(values, axis=-1, keepdims=True)
    centered = values - average
    variance = jnp.mean(centered * centered, axis=-1, keepdims=True)
    return centered * lax.rsqrt(variance + EPS) * gain


def whole(shape):
    return pl.BlockSpec(shape, lambda *_: (0,) * len(shape))


def query_kernel(half_ref, lat_ref, gain_ref, wq_ref, out_ref, q_s):
    normed = norm_rows(lat_ref[...].astype(F32), gain_ref[...]).astype(BF)
    q = jnp.dot(normed, wq_ref[...], preferred_element_type=F32).astype(BF)
    q_s[...] = q * jnp.asarray(DH ** -0.5, BF)
    rows = q_s[pl.ds(pl.multiple_of(half_ref[0] * 16, 16), 16), :]
    out_ref[...] = jnp.broadcast_to(rows[None], out_ref.shape)


def keyval_kernel(obs_ref, w_ref, up_ref, down_ref, k_ref, va_ref, mlp_ref):
    @pl.when(pl.program_id(0) == 0)
    def _():
        mlp_ref[:, :256] = up_ref[...]
        mlp_ref[:256, 256:] = down_ref[:, :256]
        mlp_ref[256:, 256:] = down_ref[:, 256:]

    kv = jnp.dot(obs_ref[...], w_ref[...], preferred_element_type=F32).astype(BF)
    k_ref[...] = kv[:, :D]
    low_half = lanes_of((kv.shape[0], 128)) < DH
    ones = jnp.ones((kv.shape[0], 128), BF)
    for p in range(H // 2):
        v = kv[:, D + 128 * p : D + 128 * (p + 1)]
        va_ref[:, 256 * p : 256 * p + 128] = jnp.where(low_half, v, ones)
        va_ref[:, 256 * p + 128 : 256 * p + 256] = jnp.where(low_half, ones, v)


def pack_stats(lse):
    lane = lanes_of(lse.shape)
    high = lse.astype(BF).astype(F32)
    rest = lse - high
    mid = rest.astype(BF).astype(F32)
    low = rest - mid
    kept = jnp.where(lane < 8, high, jnp.where(lane < 16, mid, jnp.where(lane < 24, low, 0.0)))
    return kept.astype(BF)


def attend_kernel(shift, meta_ref, vis_ref, near_ref, far_ref, k_ref, va_ref, out_ref, list_ref, q_s):
    count = meta_ref[0]
    own, core = meta_ref[1], meta_ref[2]
    column = lax.rem(meta_ref[3] - shift + NX, NX)
    seen = jnp.int32(0)
    for e in range(NZ):
        region = e * NX + column
        list_ref[seen] = jnp.int32(e)
        sees = (vis_ref[region] > 0) | (region == own)
        seen = seen + sees.astype(jnp.int32)
    last = list_ref[jnp.maximum(seen - 1, 0)]
    for k in range(3):
        list_ref[seen + k] = last

    lane = lanes_of((LR, 128))
    out_ref[:, :, :D] = jnp.zeros((NZ, LR, D), BF)
    out_ref[:, :, D:] = jnp.broadcast_to(
        jnp.where(lane < 8, NEG, 0.0).astype(BF)[None], (NZ, LR, 128)
    )

    def group(start, regions, blocks, unroll):
        keys, rows = blocks * BLK, regions * LR
        entries = [list_ref[start + k] for k in range(regions)]
        for k, e in enumerate(entries):
            region = e * NX + column
            q_s[pl.ds(pl.multiple_of(32 * k + 16 * core, 16), 16), :] = near_ref[region]
            q_s[pl.ds(pl.multiple_of(32 * k + 16 - 16 * core, 16), 16), :] = far_ref[region]
        wide = lanes_of((rows, 128))
        low_half = wide < DH
        sure = max(1, blocks // 2 + (blocks > 2))

        def pair(p, stats):
            here = pl.ds(pl.multiple_of(128 * p, 128), 128)
            even_at = pl.ds(pl.multiple_of(256 * p, 128), 128)
            odd_at = pl.ds(pl.multiple_of(256 * p + 128, 128), 128)
            qp = q_s[:rows, here]
            zero = jnp.zeros_like(qp)
            both = jnp.concatenate([jnp.where(low_half, qp, zero), jnp.where(low_half, zero, qp)], 0)
            scores = lax.dot_general(
                both, k_ref[:keys, here], (((1,), (1,)), ((), ())), preferred_element_type=F32
            )
            parts = [scores[:, : sure * BLK]]
            for j in range(sure, blocks):
                parts.append(jnp.where(count > j, scores[:, j * BLK : (j + 1) * BLK], NEG))
            scores = jnp.concatenate(parts, 1)
            peak = jnp.max(scores, axis=-1, keepdims=True)
            weights = jnp.exp(scores - peak).astype(BF)
            even = jnp.dot(weights[:rows], va_ref[:keys, even_at], preferred_element_type=F32)
            odd = jnp.dot(weights[rows:], va_ref[:keys, odd_at], preferred_element_type=F32)
            total = pltpu.roll(jnp.where(low_half, odd, even), DH, 1)
            value = (jnp.where(low_half, even, odd) / total).astype(BF)
            lse = jnp.where(low_half, peak[:rows], peak[rows:]) + jnp.log(total)
            turned = pltpu.roll(lse, DH, 1)
            within = wide & 7
            stats = jnp.where(within == 2 * p, lse, jnp.where(within == 2 * p + 1, turned, stats))
            for k, e in enumerate(entries):
                out_ref[e, :, here] = value[32 * k : 32 * (k + 1)]
            return stats

        def pairs(i, stats):
            for k in range(unroll):
                stats = pair(i * unroll + k, stats)
            return stats

        stats = lax.fori_loop(0, H // 2 // unroll, pairs, jnp.zeros((rows, 128), F32))
        packed = pack_stats(stats)
        for k, e in enumerate(entries):
            out_ref[e, :, D:] = packed[32 * k : 32 * (k + 1)]

    for least, blocks in ((1, 2), (3, 4)):

        @pl.when((count >= least) & (count <= blocks))
        def _():
            def body(g, carry):
                group(4 * g, 4, blocks, 1)
                return carry

            lax.fori_loop(0, (seen + 3) // 4, body, 0)

    for fewest, regions, unroll in ((1, 4, 1), (5, 6, 2), (7, 8, 1)):

        @pl.when((count > 4) & (seen >= fewest) & (seen <= regions))
        def _():
            group(0, regions, 8, unroll)


def attend(shift, meta, seen_by, near, far, keys, values):
    scalars = pl.BlockSpec(memory_space=pltpu.SMEM)
    vectors = pl.BlockSpec(memory_space=pltpu.VMEM)
    return pl.pallas_call(
        functools.partial(attend_kernel, shift),
        out_shape=jax.ShapeDtypeStruct((NZ, LR, WIDE), BF),
        in_specs=[scalars] * 2 + [vectors] * 4,
        out_specs=vectors,
        scratch_shapes=[pltpu.SMEM((16,), jnp.int32), pltpu.VMEM((256, D), BF)],
        compiler_params=pltpu.CompilerParams(vmem_limit_bytes=24 << 20),
        cost_estimate=pl.CostEstimate(flops=2 << 30, bytes_accessed=8 << 20, transcendentals=2 << 20),
        name="attend",
    )(meta, seen_by, near, far, keys, values)


def spread_matrix():
    row = lax.broadcasted_iota(jnp.int32, (128, WIDE), 0)
    col = lax.broadcasted_iota(jnp.int32, (128, WIDE), 1)
    head = jnp.where(col < D, col // DH, jnp.where(col < D + 24, col & 7, -1))
    return jnp.where((row < 24) & ((row & 7) == head), 1.0, 0.0).astype(BF)


def join(pieces, spread):
    lses = [jnp.dot(p[:, D:], spread, preferred_element_type=F32) for p in pieces]
    highest = functools.reduce(jnp.maximum, lses)
    scales = [jnp.exp(l - highest) for l in lses]
    total = functools.reduce(jnp.add, scales)
    value = functools.reduce(
        jnp.add, [p[:, :D].astype(F32) * s[:, :D] for p, s in zip(pieces, scales)]
    )
    return value / total[:, :D], (highest + jnp.log(total))[:, D:]


def join_kernel(*refs):
    *ins, out = refs
    pieces = [r[...] for r in ins] if len(ins) > 1 else [ins[0][k] for k in range(ins[0].shape[0])]
    value, lse = join(pieces, spread_matrix())
    out[..., :D] = jnp.broadcast_to(value.astype(BF), (*out.shape[:-1], D))
    out[..., D:] = jnp.broadcast_to(pack_stats(lse), (*out.shape[:-1], 128))


def joined(pieces, shape):
    return pl.pallas_call(
        join_kernel,
        out_shape=jax.ShapeDtypeStruct(shape, BF),
        in_specs=[pl.BlockSpec(memory_space=pltpu.VMEM)] * len(pieces),
        out_specs=pl.BlockSpec(memory_space=pltpu.VMEM),
        compiler_params=pltpu.CompilerParams(vmem_limit_bytes=16 << 20),
        name="join_pieces",
    )(*pieces)


def final_kernel(row_ref, pieces_ref, lat_ref, gain_ref, wo_ref, *refs):
    weights, (res_ref, part_ref, sums) = refs[:4], refs[4:]
    pieces = [pieces_ref[k] for k in range(8)]
    value, _ = join(pieces, spread_matrix())
    attended = value.astype(BF)
    residual = lat_ref[...].astype(F32) + jnp.dot(attended, wo_ref[...], preferred_element_type=F32)
    normed = norm_rows(residual, gain_ref[...]).astype(BF)
    res_ref[...] = residual
    for k, w in enumerate(weights):
        v = jnp.dot(normed, w[:, :256], preferred_element_type=F32)
        hidden = jax.nn.gelu(v, approximate=True).astype(BF)
        down = jnp.concatenate([w[:256, 256:], w[256:, 256:]], 1)
        sums[lax.rem(row_ref[0] - k + 4, 4)] = jnp.dot(hidden, down, preferred_element_type=F32)
    part_ref[...] = (sums[0] + sums[1]) + (sums[2] + sums[3])


def shifted_x(a, by):
    pairs = [
        (zz * NX + xx, zz * NX + (xx + by) % NX) for zz in range(NZ) for xx in range(NX)
    ]
    return lax.ppermute(a, "region", pairs) if by % NX else a


def shifted_y(a, by):
    return lax.ppermute(a, "tm", [(k, (k + 2 * by) % 8) for k in range(8)]) if by % 4 else a


def core_swapped(a):
    return lax.ppermute(a, "tm", [(k, k ^ 1) for k in range(8)])


def on_device(
    observations,
    counts,
    visible,
    latents,
    lat_gain,
    mlp_gain,
    w_query,
    w_keyval,
    w_out,
    w_up,
    w_down,
):
    own = lax.axis_index("region")
    slot = lax.axis_index("tm")
    x, row, core = own % NX, slot // 2, slot % 2
    observed = observations[0, 0]
    lat = latents[0]
    scalars = pl.BlockSpec(memory_space=pltpu.SMEM)
    vectors = pl.BlockSpec(memory_space=pltpu.VMEM)

    with jax.named_scope("queries"):
        q = pl.pallas_call(
            query_kernel,
            out_shape=jax.ShapeDtypeStruct((NZ * NX, 16, D), BF),
            in_specs=[scalars] + [vectors] * 3,
            out_specs=vectors,
            scratch_shapes=[pltpu.VMEM((LR, D), BF)],
            name="queries",
        )(core[None], lat, lat_gain[None], w_query)
    with jax.named_scope("gather"):
        near = lax.all_to_all(q, "region", 0, 0, tiled=True)

    with jax.named_scope("keyval"):
        keys, values, mlp = pl.pallas_call(
            keyval_kernel,
            grid=(observed.shape[0] // BLK,),
            out_shape=[
                jax.ShapeDtypeStruct((observed.shape[0], D), BF),
                jax.ShapeDtypeStruct((observed.shape[0], 2 * D), BF),
                jax.ShapeDtypeStruct((D, D), BF),
            ],
            in_specs=[
                pl.BlockSpec((BLK, D), lambda i: (i, 0)),
                pl.BlockSpec((D, 2 * D), lambda i: (0, 0)),
                pl.BlockSpec((D, 256), lambda i: (0, 0)),
                pl.BlockSpec((256, D), lambda i: (0, 0)),
            ],
            out_specs=[
                pl.BlockSpec((BLK, D), lambda i: (i, 0)),
                pl.BlockSpec((BLK, 2 * D), lambda i: (i, 0)),
                pl.BlockSpec((D, D), lambda i: (0, 0)),
            ],
            compiler_params=pltpu.CompilerParams(vmem_limit_bytes=58 << 20),
            cost_estimate=pl.CostEstimate(flops=2 << 30, bytes_accessed=9 << 20, transcendentals=0),
            name="keyval",
        )(observed, w_keyval, w_up, w_down)

    seen_by = lax.dynamic_slice_in_dim(visible, own, 1, 1)[:, 0]
    meta = jnp.stack([counts[0, 0], own, core, x]).astype(jnp.int32)
    near, values, seen_by, meta = lax.optimization_barrier((near, values, seen_by, meta))
    with jax.named_scope("gather"):
        far = core_swapped(near)
    with jax.named_scope("weights"):
        across = shifted_y(mlp, 2)
    with jax.named_scope("attend"):
        pieces = []
        for d in (2, 1, 3, 0):
            if d == 0:
                meta, across = lax.optimization_barrier((meta, across))
            part = attend(d, meta, seen_by, near, far, keys, values)
            pieces.append(shifted_x(part.reshape(NZ * LR, WIDE), -d))
    with jax.named_scope("join_x"):
        part = joined(pieces, (NZ * LR, WIDE)).reshape(NZ, LR, WIDE)
    part, mlp = lax.optimization_barrier((part, mlp))
    with jax.named_scope("weights"):
        shards = [mlp, shifted_y(mlp, 1), across, shifted_y(mlp, 3)]
    with jax.named_scope("join_z"):
        groups = [[zz * NX + xx for zz in range(NZ)] for xx in range(NX)]
        part = lax.all_to_all(part, "region", 0, 0, axis_index_groups=groups, tiled=True)
        part = joined([part], (8, LR, WIDE))
    with jax.named_scope("join_t"):
        pieces = lax.all_to_all(part, "tm", 0, 0, tiled=True)
    with jax.named_scope("final"):
        residual, mine = pl.pallas_call(
            final_kernel,
            out_shape=[jax.ShapeDtypeStruct((LR, D), F32)] * 2,
            in_specs=[scalars] + [vectors] * 8,
            out_specs=[vectors] * 2,
            scratch_shapes=[pltpu.VMEM((4, LR, D), F32)],
            compiler_params=pltpu.CompilerParams(vmem_limit_bytes=16 << 20),
            name="final",
        )(row[None], pieces, lat, mlp_gain[None], w_out, *shards)
        out = residual + (mine + core_swapped(mine))
    return out.astype(BF)[None]


def solution(mesh):
    placed = (
        P("region", "tm", None, None),
        P("region", "tm"),
        P(),
        P("region", None, None),
        P(),
        P(),
        P(),
        P(),
        P(),
        P(None, "tm"),
        P("tm", None),
    )
    return jax.shard_map(
        on_device, mesh=mesh, in_specs=placed, out_specs=P("region", None, None), check_vma=False
    )
```

```python
import functools

import jax
import jax.numpy as jnp
from jax import lax
from jax.experimental import pallas as pl
from jax.experimental.pallas import tpu as pltpu
from jax.sharding import PartitionSpec as P

H = 8
BLK = 256
NZ, NX = 8, 4
EPS = 1e-05
NEG = -1e30
D = 512
DH = 64
LR = 32
WIDE = D + 128
BF = jnp.bfloat16
F32 = jnp.float32


def lanes_of(shape):
    return lax.broadcasted_iota(jnp.int32, shape, len(shape) - 1)


def norm_rows(values, gain):
    average = jnp.mean(values, axis=-1, keepdims=True)
    centered = values - average
    variance = jnp.mean(centered * centered, axis=-1, keepdims=True)
    return centered * lax.rsqrt(variance + EPS) * gain


def whole(shape):
    return pl.BlockSpec(shape, lambda *_: (0,) * len(shape))


def query_kernel(half_ref, lat_ref, gain_ref, wq_ref, out_ref, q_s):
    normed = norm_rows(lat_ref[...].astype(F32), gain_ref[...]).astype(BF)
    q = jnp.dot(normed, wq_ref[...], preferred_element_type=F32).astype(BF)
    q_s[...] = q * jnp.asarray(DH ** -0.5, BF)
    rows = q_s[pl.ds(pl.multiple_of(half_ref[0] * 16, 16), 16), :]
    out_ref[...] = jnp.broadcast_to(rows[None], out_ref.shape)


def keyval_kernel(obs_ref, w_ref, up_ref, down_ref, k_ref, va_ref, mlp_ref):
    @pl.when(pl.program_id(0) == 0)
    def _():
        mlp_ref[:, :256] = up_ref[...]
        mlp_ref[:256, 256:] = down_ref[:, :256]
        mlp_ref[256:, 256:] = down_ref[:, 256:]

    kv = jnp.dot(obs_ref[...], w_ref[...], preferred_element_type=F32).astype(BF)
    k_ref[...] = kv[:, :D]
    low_half = lanes_of((kv.shape[0], 128)) < DH
    ones = jnp.ones((kv.shape[0], 128), BF)
    for p in range(H // 2):
        v = kv[:, D + 128 * p : D + 128 * (p + 1)]
        va_ref[:, 256 * p : 256 * p + 128] = jnp.where(low_half, v, ones)
        va_ref[:, 256 * p + 128 : 256 * p + 256] = jnp.where(low_half, ones, v)


def pack_stats(lse):
    lane = lanes_of(lse.shape)
    high = lse.astype(BF).astype(F32)
    rest = lse - high
    mid = rest.astype(BF).astype(F32)
    low = rest - mid
    kept = jnp.where(lane < 8, high, jnp.where(lane < 16, mid, jnp.where(lane < 24, low, 0.0)))
    return kept.astype(BF)


def attend_kernel(shifts, meta_ref, vis_ref, near_ref, far_ref, k_ref, va_ref, *rest):
    outs = rest[: len(shifts)]
    list_ref, q_s, out_ref = rest[len(shifts) :]
    count = meta_ref[0]
    own, core = meta_ref[1], meta_ref[2]
    seen = jnp.int32(0)
    for j, shift in enumerate(shifts):
        column = lax.rem(meta_ref[3] - shift + NX, NX)
        for e in range(NZ):
            region = e * NX + column
            list_ref[0, seen] = region
            list_ref[1, seen] = jnp.int32(j * NZ + e)
            sees = (vis_ref[region] > 0) | (region == own)
            seen = seen + sees.astype(jnp.int32)
    last = jnp.maximum(seen - 1, 0)
    for k in range(4):
        for row in range(2):
            list_ref[row, seen + k] = list_ref[row, last]

    lane = lanes_of((LR, 128))
    cells = NZ * len(shifts)
    out_ref[:, :, :D] = jnp.zeros((cells, LR, D), BF)
    out_ref[:, :, D:] = jnp.broadcast_to(
        jnp.where(lane < 8, NEG, 0.0).astype(BF)[None], (cells, LR, 128)
    )

    def group(start, regions, blocks, unroll):
        keys, rows = blocks * BLK, regions * LR
        entries = [list_ref[1, start + k] for k in range(regions)]
        for k in range(regions):
            region = list_ref[0, start + k]
            q_s[pl.ds(pl.multiple_of(32 * k + 16 * core, 16), 16), :] = near_ref[region]
            q_s[pl.ds(pl.multiple_of(32 * k + 16 - 16 * core, 16), 16), :] = far_ref[region]
        wide = lanes_of((rows, 128))
        low_half = wide < DH
        sure = max(1, blocks // 2 + (blocks > 2))

        def pair(p, stats):
            here = pl.ds(pl.multiple_of(128 * p, 128), 128)
            even_at = pl.ds(pl.multiple_of(256 * p, 128), 128)
            odd_at = pl.ds(pl.multiple_of(256 * p + 128, 128), 128)
            qp = q_s[:rows, here]
            zero = jnp.zeros_like(qp)
            both = jnp.concatenate([jnp.where(low_half, qp, zero), jnp.where(low_half, zero, qp)], 0)
            scores = lax.dot_general(
                both, k_ref[:keys, here], (((1,), (1,)), ((), ())), preferred_element_type=F32
            )
            parts = [scores[:, : sure * BLK]]
            for j in range(sure, blocks):
                parts.append(jnp.where(count > j, scores[:, j * BLK : (j + 1) * BLK], NEG))
            scores = jnp.concatenate(parts, 1)
            peak = jnp.max(scores, axis=-1, keepdims=True)
            weights = jnp.exp(scores - peak).astype(BF)
            even = jnp.dot(weights[:rows], va_ref[:keys, even_at], preferred_element_type=F32)
            odd = jnp.dot(weights[rows:], va_ref[:keys, odd_at], preferred_element_type=F32)
            total = pltpu.roll(jnp.where(low_half, odd, even), DH, 1)
            value = (jnp.where(low_half, even, odd) / total).astype(BF)
            lse = jnp.where(low_half, peak[:rows], peak[rows:]) + jnp.log(total)
            turned = pltpu.roll(lse, DH, 1)
            within = wide & 7
            stats = jnp.where(within == 2 * p, lse, jnp.where(within == 2 * p + 1, turned, stats))
            for k, e in enumerate(entries):
                out_ref[e, :, here] = value[32 * k : 32 * (k + 1)]
            return stats

        def pairs(i, stats):
            for k in range(unroll):
                stats = pair(i * unroll + k, stats)
            return stats

        stats = lax.fori_loop(0, H // 2 // unroll, pairs, jnp.zeros((rows, 128), F32))
        packed = pack_stats(stats)
        for k, e in enumerate(entries):
            out_ref[e, :, D:] = packed[32 * k : 32 * (k + 1)]

    for least, blocks in ((1, 2), (3, 4)):

        @pl.when((count >= least) & (count <= blocks))
        def _():
            def body(g, carry):
                group(4 * g, 4, blocks, 1)
                return carry

            lax.fori_loop(0, (seen + 3) // 4, body, 0)

    sizes = ((4, 1), (6, 2), (8, 1)) if len(shifts) == 1 else ((8, 1), (10, 1), (12, 1), (16, 1))
    for below, (regions, unroll) in zip([0] + [r for r, _ in sizes], sizes):

        @pl.when((count > 4) & (seen > below) & (seen <= regions))
        def _():
            group(0, regions, 8, unroll)

    for j, out in enumerate(outs):
        out[...] = out_ref[NZ * j : NZ * (j + 1)]


def attend(shifts, meta, seen_by, near, far, keys, values):
    scalars = pl.BlockSpec(memory_space=pltpu.SMEM)
    vectors = pl.BlockSpec(memory_space=pltpu.VMEM)
    cells = NZ * len(shifts)
    return pl.pallas_call(
        functools.partial(attend_kernel, shifts),
        out_shape=[jax.ShapeDtypeStruct((NZ, LR, WIDE), BF)] * len(shifts),
        in_specs=[scalars] * 2 + [vectors] * 4,
        out_specs=[vectors] * len(shifts),
        scratch_shapes=[
            pltpu.SMEM((2, 24), jnp.int32),
            pltpu.VMEM((cells * LR, D), BF),
            pltpu.VMEM((cells, LR, WIDE), BF),
        ],
        compiler_params=pltpu.CompilerParams(vmem_limit_bytes=32 << 20),
        cost_estimate=pl.CostEstimate(
            flops=2 << 30, bytes_accessed=8 << 20, transcendentals=2 << 20
        ),
        name="attend",
    )(meta, seen_by, near, far, keys, values)


def spread_matrix():
    row = lax.broadcasted_iota(jnp.int32, (128, WIDE), 0)
    col = lax.broadcasted_iota(jnp.int32, (128, WIDE), 1)
    head = jnp.where(col < D, col // DH, jnp.where(col < D + 24, col & 7, -1))
    return jnp.where((row < 24) & ((row & 7) == head), 1.0, 0.0).astype(BF)


def join(pieces, spread):
    lses = [jnp.dot(p[:, D:], spread, preferred_element_type=F32) for p in pieces]
    highest = functools.reduce(jnp.maximum, lses)
    scales = [jnp.exp(l - highest) for l in lses]
    total = functools.reduce(jnp.add, scales)
    value = functools.reduce(
        jnp.add, [p[:, :D].astype(F32) * s[:, :D] for p, s in zip(pieces, scales)]
    )
    return value / total[:, :D], (highest + jnp.log(total))[:, D:]


def join_kernel(*refs):
    *ins, out = refs
    pieces = [r[...] for r in ins] if len(ins) > 1 else [ins[0][k] for k in range(ins[0].shape[0])]
    value, lse = join(pieces, spread_matrix())
    out[..., :D] = jnp.broadcast_to(value.astype(BF), (*out.shape[:-1], D))
    out[..., D:] = jnp.broadcast_to(pack_stats(lse), (*out.shape[:-1], 128))


def joined(pieces, shape):
    return pl.pallas_call(
        join_kernel,
        out_shape=jax.ShapeDtypeStruct(shape, BF),
        in_specs=[pl.BlockSpec(memory_space=pltpu.VMEM)] * len(pieces),
        out_specs=pl.BlockSpec(memory_space=pltpu.VMEM),
        compiler_params=pltpu.CompilerParams(vmem_limit_bytes=16 << 20),
        name="join_pieces",
    )(*pieces)


def final_kernel(row_ref, pieces_ref, lat_ref, gain_ref, wo_ref, *refs):
    weights, (res_ref, part_ref, sums) = refs[:4], refs[4:]
    pieces = [pieces_ref[k] for k in range(8)]
    value, _ = join(pieces, spread_matrix())
    attended = value.astype(BF)
    residual = lat_ref[...].astype(F32) + jnp.dot(attended, wo_ref[...], preferred_element_type=F32)
    normed = norm_rows(residual, gain_ref[...]).astype(BF)
    res_ref[...] = residual
    for k, w in enumerate(weights):
        v = jnp.dot(normed, w[:, :256], preferred_element_type=F32)
        hidden = jax.nn.gelu(v, approximate=True).astype(BF)
        down = jnp.concatenate([w[:256, 256:], w[256:, 256:]], 1)
        sums[lax.rem(row_ref[0] - k + 4, 4)] = jnp.dot(hidden, down, preferred_element_type=F32)
    part_ref[...] = (sums[0] + sums[1]) + (sums[2] + sums[3])


def shifted_x(a, by):
    pairs = [
        (zz * NX + xx, zz * NX + (xx + by) % NX) for zz in range(NZ) for xx in range(NX)
    ]
    return lax.ppermute(a, "region", pairs) if by % NX else a


def shifted_y(a, by):
    return lax.ppermute(a, "tm", [(k, (k + 2 * by) % 8) for k in range(8)]) if by % 4 else a


def core_swapped(a):
    return lax.ppermute(a, "tm", [(k, k ^ 1) for k in range(8)])


def on_device(
    observations,
    counts,
    visible,
    latents,
    lat_gain,
    mlp_gain,
    w_query,
    w_keyval,
    w_out,
    w_up,
    w_down,
):
    own = lax.axis_index("region")
    slot = lax.axis_index("tm")
    x, row, core = own % NX, slot // 2, slot % 2
    observed = observations[0, 0]
    lat = latents[0]
    scalars = pl.BlockSpec(memory_space=pltpu.SMEM)
    vectors = pl.BlockSpec(memory_space=pltpu.VMEM)

    with jax.named_scope("queries"):
        q = pl.pallas_call(
            query_kernel,
            out_shape=jax.ShapeDtypeStruct((NZ * NX, 16, D), BF),
            in_specs=[scalars] + [vectors] * 3,
            out_specs=vectors,
            scratch_shapes=[pltpu.VMEM((LR, D), BF)],
            name="queries",
        )(core[None], lat, lat_gain[None], w_query)
    with jax.named_scope("gather"):
        near = lax.all_to_all(q, "region", 0, 0, tiled=True)

    with jax.named_scope("keyval"):
        keys, values, mlp = pl.pallas_call(
            keyval_kernel,
            grid=(observed.shape[0] // BLK,),
            out_shape=[
                jax.ShapeDtypeStruct((observed.shape[0], D), BF),
                jax.ShapeDtypeStruct((observed.shape[0], 2 * D), BF),
                jax.ShapeDtypeStruct((D, D), BF),
            ],
            in_specs=[
                pl.BlockSpec((BLK, D), lambda i: (i, 0)),
                pl.BlockSpec((D, 2 * D), lambda i: (0, 0)),
                pl.BlockSpec((D, 256), lambda i: (0, 0)),
                pl.BlockSpec((256, D), lambda i: (0, 0)),
            ],
            out_specs=[
                pl.BlockSpec((BLK, D), lambda i: (i, 0)),
                pl.BlockSpec((BLK, 2 * D), lambda i: (i, 0)),
                pl.BlockSpec((D, D), lambda i: (0, 0)),
            ],
            compiler_params=pltpu.CompilerParams(vmem_limit_bytes=58 << 20),
            cost_estimate=pl.CostEstimate(flops=2 << 30, bytes_accessed=9 << 20, transcendentals=0),
            name="keyval",
        )(observed, w_keyval, w_up, w_down)

    seen_by = lax.dynamic_slice_in_dim(visible, own, 1, 1)[:, 0]
    meta = jnp.stack([counts[0, 0], own, core, x]).astype(jnp.int32)
    near, values, seen_by, meta = lax.optimization_barrier((near, values, seen_by, meta))
    with jax.named_scope("gather"):
        far = core_swapped(near)
    with jax.named_scope("weights"):
        shards = [shifted_y(mlp, k) for k in range(4)]

    with jax.named_scope("attend"):
        pieces = []
        for shifts in ((2,), (1, 3), (0,)):
            if shifts == (0,):
                meta, *shards = lax.optimization_barrier((meta, *shards))
            parts = attend(shifts, meta, seen_by, near, far, keys, values)
            for d, part in zip(shifts, parts):
                pieces.append(shifted_x(part.reshape(NZ * LR, WIDE), -d))
    with jax.named_scope("join_x"):
        part = joined(pieces, (NZ * LR, WIDE)).reshape(NZ, LR, WIDE)
    with jax.named_scope("join_z"):
        groups = [[zz * NX + xx for zz in range(NZ)] for xx in range(NX)]
        part = lax.all_to_all(part, "region", 0, 0, axis_index_groups=groups, tiled=True)
        part = joined([part], (8, LR, WIDE))
    with jax.named_scope("join_t"):
        pieces = lax.all_to_all(part, "tm", 0, 0, tiled=True)
    with jax.named_scope("final"):
        residual, mine = pl.pallas_call(
            final_kernel,
            out_shape=[jax.ShapeDtypeStruct((LR, D), F32)] * 2,
            in_specs=[scalars] + [vectors] * 8,
            out_specs=[vectors] * 2,
            scratch_shapes=[pltpu.VMEM((4, LR, D), F32)],
            compiler_params=pltpu.CompilerParams(vmem_limit_bytes=16 << 20),
            name="final",
        )(row[None], pieces, lat, mlp_gain[None], w_out, *shards)
        out = residual + (mine + core_swapped(mine))
    return out.astype(BF)[None]


def solution(mesh):
    placed = (
        P("region", "tm", None, None),
        P("region", "tm"),
        P(),
        P("region", None, None),
        P(),
        P(),
        P(),
        P(),
        P(),
        P(None, "tm"),
        P("tm", None),
    )
    return jax.shard_map(
        on_device, mesh=mesh, in_specs=placed, out_specs=P("region", None, None), check_vma=False
    )
```

```python
import functools

import jax
import jax.numpy as jnp
from jax import lax
from jax.experimental import pallas as pl
from jax.experimental.pallas import tpu as pltpu
from jax.sharding import PartitionSpec as P

H = 8
BLK = 256
NZ, NX = 8, 4
EPS = 1e-05
NEG = -1e30
D = 512
DH = 64
LR = 32
WIDE = D + 128
BF = jnp.bfloat16
F32 = jnp.float32


def lanes_of(shape):
    return lax.broadcasted_iota(jnp.int32, shape, len(shape) - 1)


def norm_rows(values, gain):
    average = jnp.mean(values, axis=-1, keepdims=True)
    centered = values - average
    variance = jnp.mean(centered * centered, axis=-1, keepdims=True)
    return centered * lax.rsqrt(variance + EPS) * gain


def whole(shape):
    return pl.BlockSpec(shape, lambda *_: (0,) * len(shape))


def query_kernel(half_ref, lat_ref, gain_ref, wq_ref, out_ref, q_s):
    normed = norm_rows(lat_ref[...].astype(F32), gain_ref[...]).astype(BF)
    q = jnp.dot(normed, wq_ref[...], preferred_element_type=F32).astype(BF)
    q_s[...] = q * jnp.asarray(DH ** -0.5, BF)
    rows = q_s[pl.ds(pl.multiple_of(half_ref[0] * 16, 16), 16), :]
    out_ref[...] = jnp.broadcast_to(rows[None], out_ref.shape)


def keyval_kernel(obs_ref, w_ref, up_ref, down_ref, k_ref, va_ref, mlp_ref):
    @pl.when(pl.program_id(0) == 0)
    def _():
        mlp_ref[:, :256] = up_ref[...]
        mlp_ref[:256, 256:] = down_ref[:, :256]
        mlp_ref[256:, 256:] = down_ref[:, 256:]

    kv = jnp.dot(obs_ref[...], w_ref[...], preferred_element_type=F32).astype(BF)
    k_ref[...] = kv[:, :D]
    low_half = lanes_of((kv.shape[0], 128)) < DH
    ones = jnp.ones((kv.shape[0], 128), BF)
    for p in range(H // 2):
        v = kv[:, D + 128 * p : D + 128 * (p + 1)]
        va_ref[:, 256 * p : 256 * p + 128] = jnp.where(low_half, v, ones)
        va_ref[:, 256 * p + 128 : 256 * p + 256] = jnp.where(low_half, ones, v)


def pack_stats(lse):
    lane = lanes_of(lse.shape)
    high = lse.astype(BF).astype(F32)
    rest = lse - high
    mid = rest.astype(BF).astype(F32)
    low = rest - mid
    kept = jnp.where(lane < 8, high, jnp.where(lane < 16, mid, jnp.where(lane < 24, low, 0.0)))
    return kept.astype(BF)


def attend_kernel(shifts, meta_ref, vis_ref, near_ref, far_ref, k_ref, va_ref, *rest):
    outs = rest[: len(shifts)]
    list_ref, q_s, out_ref = rest[len(shifts) :]
    count = meta_ref[0]
    own, core = meta_ref[1], meta_ref[2]
    seen = jnp.int32(0)
    for j, shift in enumerate(shifts):
        column = lax.rem(meta_ref[3] - shift + NX, NX)
        for e in range(NZ):
            region = e * NX + column
            list_ref[0, seen] = region
            list_ref[1, seen] = jnp.int32(j * NZ + e)
            sees = (vis_ref[region] > 0) | (region == own)
            seen = seen + sees.astype(jnp.int32)
    last = jnp.maximum(seen - 1, 0)
    for k in range(7):
        for row in range(2):
            list_ref[row, seen + k] = list_ref[row, last]

    lane = lanes_of((LR, 128))
    cells = NZ * len(shifts)
    out_ref[:, :, :D] = jnp.zeros((cells, LR, D), BF)
    out_ref[:, :, D:] = jnp.broadcast_to(
        jnp.where(lane < 8, NEG, 0.0).astype(BF)[None], (cells, LR, 128)
    )

    def group(start, regions, blocks, unroll):
        keys, rows = blocks * BLK, regions * LR
        entries = [list_ref[1, start + k] for k in range(regions)]
        for k in range(regions):
            region = list_ref[0, start + k]
            q_s[pl.ds(pl.multiple_of(32 * k + 16 * core, 16), 16), :] = near_ref[region]
            q_s[pl.ds(pl.multiple_of(32 * k + 16 - 16 * core, 16), 16), :] = far_ref[region]
        wide = lanes_of((rows, 128))
        low_half = wide < DH
        sure = max(1, blocks // 2 + (blocks > 2))

        def pair(p, stats):
            here = pl.ds(pl.multiple_of(128 * p, 128), 128)
            even_at = pl.ds(pl.multiple_of(256 * p, 128), 128)
            odd_at = pl.ds(pl.multiple_of(256 * p + 128, 128), 128)
            qp = q_s[:rows, here]
            zero = jnp.zeros_like(qp)
            both = jnp.concatenate([jnp.where(low_half, qp, zero), jnp.where(low_half, zero, qp)], 0)
            scores = lax.dot_general(
                both, k_ref[:keys, here], (((1,), (1,)), ((), ())), preferred_element_type=F32
            )
            parts = [scores[:, : sure * BLK]]
            for j in range(sure, blocks):
                parts.append(jnp.where(count > j, scores[:, j * BLK : (j + 1) * BLK], NEG))
            scores = jnp.concatenate(parts, 1)
            peak = jnp.max(scores, axis=-1, keepdims=True)
            weights = jnp.exp(scores - peak).astype(BF)
            even = jnp.dot(weights[:rows], va_ref[:keys, even_at], preferred_element_type=F32)
            odd = jnp.dot(weights[rows:], va_ref[:keys, odd_at], preferred_element_type=F32)
            total = pltpu.roll(jnp.where(low_half, odd, even), DH, 1)
            value = (jnp.where(low_half, even, odd) / total).astype(BF)
            lse = jnp.where(low_half, peak[:rows], peak[rows:]) + jnp.log(total)
            turned = pltpu.roll(lse, DH, 1)
            within = wide & 7
            stats = jnp.where(within == 2 * p, lse, jnp.where(within == 2 * p + 1, turned, stats))
            for k, e in enumerate(entries):
                out_ref[e, :, here] = value[32 * k : 32 * (k + 1)]
            return stats

        def pairs(i, stats):
            for k in range(unroll):
                stats = pair(i * unroll + k, stats)
            return stats

        stats = lax.fori_loop(0, H // 2 // unroll, pairs, jnp.zeros((rows, 128), F32))
        packed = pack_stats(stats)
        for k, e in enumerate(entries):
            out_ref[e, :, D:] = packed[32 * k : 32 * (k + 1)]

    for least, blocks in ((1, 2), (3, 4)):

        @pl.when((count >= least) & (count <= blocks))
        def _():
            def body(g, carry):
                group(4 * g, 4, blocks, 1)
                return carry

            lax.fori_loop(0, (seen + 3) // 4, body, 0)

    sizes = ((4, 1), (6, 2), (8, 1)) if len(shifts) == 1 else ((8, 1), (10, 1), (12, 1), (16, 1))
    for below, (regions, unroll) in zip([0] + [r for r, _ in sizes], sizes):

        @pl.when((count > 4) & (seen > below) & (seen <= regions))
        def _():
            group(0, regions, 8, unroll)

    for j, out in enumerate(outs):
        out[...] = out_ref[NZ * j : NZ * (j + 1)]


def attend(shifts, meta, seen_by, near, far, keys, values):
    scalars = pl.BlockSpec(memory_space=pltpu.SMEM)
    vectors = pl.BlockSpec(memory_space=pltpu.VMEM)
    cells = NZ * len(shifts)
    return pl.pallas_call(
        functools.partial(attend_kernel, shifts),
        out_shape=[jax.ShapeDtypeStruct((NZ, LR, WIDE), BF)] * len(shifts),
        in_specs=[scalars] * 2 + [vectors] * 4,
        out_specs=[vectors] * len(shifts),
        scratch_shapes=[
            pltpu.SMEM((2, 24), jnp.int32),
            pltpu.VMEM((cells * LR, D), BF),
            pltpu.VMEM((cells, LR, WIDE), BF),
        ],
        compiler_params=pltpu.CompilerParams(vmem_limit_bytes=32 << 20),
        cost_estimate=pl.CostEstimate(
            flops=2 << 30, bytes_accessed=8 << 20, transcendentals=2 << 20
        ),
        name="attend",
    )(meta, seen_by, near, far, keys, values)


def spread_matrix():
    row = lax.broadcasted_iota(jnp.int32, (128, WIDE), 0)
    col = lax.broadcasted_iota(jnp.int32, (128, WIDE), 1)
    head = jnp.where(col < D, col // DH, jnp.where(col < D + 24, col & 7, -1))
    return jnp.where((row < 24) & ((row & 7) == head), 1.0, 0.0).astype(BF)


def join(pieces, spread):
    lses = [jnp.dot(p[:, D:], spread, preferred_element_type=F32) for p in pieces]
    highest = functools.reduce(jnp.maximum, lses)
    scales = [jnp.exp(l - highest) for l in lses]
    total = functools.reduce(jnp.add, scales)
    value = functools.reduce(
        jnp.add, [p[:, :D].astype(F32) * s[:, :D] for p, s in zip(pieces, scales)]
    )
    return value / total[:, :D], (highest + jnp.log(total))[:, D:]


def join_kernel(*refs):
    *ins, out = refs
    pieces = [r[...] for r in ins] if len(ins) > 1 else [ins[0][k] for k in range(ins[0].shape[0])]
    value, lse = join(pieces, spread_matrix())
    out[..., :D] = jnp.broadcast_to(value.astype(BF), (*out.shape[:-1], D))
    out[..., D:] = jnp.broadcast_to(pack_stats(lse), (*out.shape[:-1], 128))


def joined(pieces, shape):
    return pl.pallas_call(
        join_kernel,
        out_shape=jax.ShapeDtypeStruct(shape, BF),
        in_specs=[pl.BlockSpec(memory_space=pltpu.VMEM)] * len(pieces),
        out_specs=pl.BlockSpec(memory_space=pltpu.VMEM),
        compiler_params=pltpu.CompilerParams(vmem_limit_bytes=16 << 20),
        name="join_pieces",
    )(*pieces)


def final_kernel(row_ref, pieces_ref, lat_ref, gain_ref, wo_ref, *refs):
    weights, (res_ref, part_ref, sums) = refs[:4], refs[4:]
    pieces = [pieces_ref[k] for k in range(8)]
    value, _ = join(pieces, spread_matrix())
    attended = value.astype(BF)
    residual = lat_ref[...].astype(F32) + jnp.dot(attended, wo_ref[...], preferred_element_type=F32)
    normed = norm_rows(residual, gain_ref[...]).astype(BF)
    res_ref[...] = residual
    for k, w in enumerate(weights):
        v = jnp.dot(normed, w[:, :256], preferred_element_type=F32)
        hidden = jax.nn.gelu(v, approximate=True).astype(BF)
        down = jnp.concatenate([w[:256, 256:], w[256:, 256:]], 1)
        sums[lax.rem(row_ref[0] - k + 4, 4)] = jnp.dot(hidden, down, preferred_element_type=F32)
    part_ref[...] = (sums[0] + sums[1]) + (sums[2] + sums[3])


def shifted_x(a, by):
    pairs = [
        (zz * NX + xx, zz * NX + (xx + by) % NX) for zz in range(NZ) for xx in range(NX)
    ]
    return lax.ppermute(a, "region", pairs) if by % NX else a


def shifted_y(a, by):
    return lax.ppermute(a, "tm", [(k, (k + 2 * by) % 8) for k in range(8)]) if by % 4 else a


def core_swapped(a):
    return lax.ppermute(a, "tm", [(k, k ^ 1) for k in range(8)])


def on_device(
    observations,
    counts,
    visible,
    latents,
    lat_gain,
    mlp_gain,
    w_query,
    w_keyval,
    w_out,
    w_up,
    w_down,
):
    own = lax.axis_index("region")
    slot = lax.axis_index("tm")
    x, row, core = own % NX, slot // 2, slot % 2
    observed = observations[0, 0]
    lat = latents[0]
    scalars = pl.BlockSpec(memory_space=pltpu.SMEM)
    vectors = pl.BlockSpec(memory_space=pltpu.VMEM)

    with jax.named_scope("queries"):
        q = pl.pallas_call(
            query_kernel,
            out_shape=jax.ShapeDtypeStruct((NZ * NX, 16, D), BF),
            in_specs=[scalars] + [vectors] * 3,
            out_specs=vectors,
            scratch_shapes=[pltpu.VMEM((LR, D), BF)],
            name="queries",
        )(core[None], lat, lat_gain[None], w_query)
    with jax.named_scope("gather"):
        near = lax.all_to_all(q, "region", 0, 0, tiled=True)

    with jax.named_scope("keyval"):
        keys, values, mlp = pl.pallas_call(
            keyval_kernel,
            grid=(observed.shape[0] // BLK,),
            out_shape=[
                jax.ShapeDtypeStruct((observed.shape[0], D), BF),
                jax.ShapeDtypeStruct((observed.shape[0], 2 * D), BF),
                jax.ShapeDtypeStruct((D, D), BF),
            ],
            in_specs=[
                pl.BlockSpec((BLK, D), lambda i: (i, 0)),
                pl.BlockSpec((D, 2 * D), lambda i: (0, 0)),
                pl.BlockSpec((D, 256), lambda i: (0, 0)),
                pl.BlockSpec((256, D), lambda i: (0, 0)),
            ],
            out_specs=[
                pl.BlockSpec((BLK, D), lambda i: (i, 0)),
                pl.BlockSpec((BLK, 2 * D), lambda i: (i, 0)),
                pl.BlockSpec((D, D), lambda i: (0, 0)),
            ],
            compiler_params=pltpu.CompilerParams(vmem_limit_bytes=58 << 20),
            cost_estimate=pl.CostEstimate(flops=2 << 30, bytes_accessed=9 << 20, transcendentals=0),
            name="keyval",
        )(observed, w_keyval, w_up, w_down)

    seen_by = lax.dynamic_slice_in_dim(visible, own, 1, 1)[:, 0]
    meta = jnp.stack([counts[0, 0], own, core, x]).astype(jnp.int32)
    near, values, seen_by, meta = lax.optimization_barrier((near, values, seen_by, meta))
    with jax.named_scope("gather"):
        far = core_swapped(near)
    with jax.named_scope("weights"):
        shards = [shifted_y(mlp, k) for k in range(4)]

    with jax.named_scope("attend"):
        pieces = []
        for shifts in ((2,), (1, 3), (0,)):
            if shifts == (0,):
                meta, *shards = lax.optimization_barrier((meta, *shards))
            parts = attend(shifts, meta, seen_by, near, far, keys, values)
            for d, part in zip(shifts, parts):
                pieces.append(shifted_x(part.reshape(NZ * LR, WIDE), -d))
    with jax.named_scope("join_x"):
        part = joined(pieces, (NZ * LR, WIDE)).reshape(NZ, LR, WIDE)
    with jax.named_scope("join_z"):
        groups = [[zz * NX + xx for zz in range(NZ)] for xx in range(NX)]
        part = lax.all_to_all(part, "region", 0, 0, axis_index_groups=groups, tiled=True)
        part = joined([part], (8, LR, WIDE))
    with jax.named_scope("join_t"):
        pieces = lax.all_to_all(part, "tm", 0, 0, tiled=True)
    with jax.named_scope("final"):
        residual, mine = pl.pallas_call(
            final_kernel,
            out_shape=[jax.ShapeDtypeStruct((LR, D), F32)] * 2,
            in_specs=[scalars] + [vectors] * 8,
            out_specs=[vectors] * 2,
            scratch_shapes=[pltpu.VMEM((4, LR, D), F32)],
            compiler_params=pltpu.CompilerParams(vmem_limit_bytes=16 << 20),
            name="final",
        )(row[None], pieces, lat, mlp_gain[None], w_out, *shards)
        out = residual + (mine + core_swapped(mine))
    return out.astype(BF)[None]


def solution(mesh):
    placed = (
        P("region", "tm", None, None),
        P("region", "tm"),
        P(),
        P("region", None, None),
        P(),
        P(),
        P(),
        P(),
        P(),
        P(None, "tm"),
        P("tm", None),
    )
    return jax.shard_map(
        on_device, mesh=mesh, in_specs=placed, out_specs=P("region", None, None), check_vma=False
    )
```
